32 devices in a mesh: pipe: 4 (over y, x), expert: 8 (over z, core).
Axes of the slice: x: 2, y: 2, z: 4, core: 2. Of those that a mesh axis runs over, the one named last changes fastest.
Arguments:
- handoff: bfloat16 [4, 1024, 2048], P('pipe', 'expert'), may hold values from -6 to 6
- saved_in: bfloat16 [4, 1024, 2048], P('pipe', 'expert'), may hold values from -6 to 6
- grad_handoff: bfloat16 [4, 1024, 2048], P('pipe', 'expert'), may hold values from -6 to 6
- route_fwd: int32 [4, 1024, 2], P('pipe', 'expert'), may hold values from 0 to 3, all different within a row; in each aligned block of 128 rows (0 to 127, 128 to 255, ..., all dimensions but the last counted through in order) at most 96 rows name the same one
- route_bwd: int32 [4, 1024, 2], P('pipe', 'expert'), may hold values from 0 to 3, all different within a row; in each aligned block of 128 rows (0 to 127, 128 to 255, ..., all dimensions but the last counted through in order) at most 96 rows name the same one
- norm_gain: float32 [4, 2048], P('pipe'), may hold values from 0.6 to 4.2, as said below
- router: bfloat16 [4, 2048, 4], P('pipe'), may hold values from -0.125 to 0.125
- up_proj: bfloat16 [4, 2048, 2048], P('pipe', None, 'expert'), may hold values from -0.125 to 0.125
- down_proj: bfloat16 [4, 2048, 2048], P('pipe', 'expert'), may hold values from -0.25 to 0.25
- moment_m: float32 [4, 2048, 4], P('pipe', 'expert'), may hold values from -0.006 to 0.006
- moment_v: float32 [4, 2048, 4], P('pipe', 'expert'), may hold values from 1e-07 to 4e-06
Outputs:
- segment_out: bfloat16 [4, 1024, 2048], P('pipe', 'expert')
- grad_back: bfloat16 [4, 1024, 2048], P('pipe', 'expert')
- new_m: float32 [4, 2048, 4], P('pipe', 'expert')
- new_v: float32 [4, 2048, 4], P('pipe', 'expert')
- router_update: float32 [4, 2048, 4], P('pipe', 'expert')
The draws below stay inside these ranges and needn't reach their ends.
Inputs may be any that keep to these rules, and one draw needn't show every extreme that they name: `route_fwd`: each token names two different experts. In the rows of one device no expert is named more than 96 times, a bound that some block reaches in every draw. `route_bwd`: each token names two different experts. In the rows of one device no expert is named more than 96 times, a bound that some block reaches in every draw. `norm_gain`: Positive.
All inputs are finite; a program needn't handle non-finite values.
Results may differ from the reference program's by a relative error of at most 0.0075.
Values may be sent and summed in bfloat16 or wider, within the bound.
No kernel may reach another device: no remote copies, remote signals or barrier semaphores. Data moves between devices by JAX's collectives and lax.ppermute only.
A program may use at most 128 MiB of HBM per device.

```python
import math
import jax
import jax.numpy as jnp
import numpy as np
from jax import lax

D = 2048
FF = 512
TOK_DEV = 128
STEP = 10
SECTIONS = 4
EXPERTS = 4
CAP = 96
TOKENS = 1024
MOST_ROWS = 768


def draw_norm_gain(key, part):
    rising = 1.0 + 2.0 * jnp.arange(D, dtype=jnp.float32) / (D - 1)
    spread = jax.random.uniform(key, (SECTIONS, D), jnp.float32, 0.8, 1.2)
    return rising[None, :] * spread


def spiked(entries, key, source, target, blocks, factor):
    owner, partner = [(jnp.arange(entries.shape[axis_at]) // (entries.shape[axis_at] // blocks)).reshape([-1 if axis == axis_at else 1 for axis in range(entries.ndim)]) for axis_at in (source, target)]
    chosen = jax.random.permutation(key, blocks)[partner]
    strong = (owner == chosen) | (owner == (partner + blocks // 2) % blocks)
    return jnp.where(strong, factor * entries, entries)


def levels(rng, extent, split, smallest, largest):
    gain, own = 1.0, jax.random.fold_in(rng, 6)
    for position, shards_of in split:
        draws = jnp.exp(jax.random.uniform(jax.random.fold_in(own, position), (shards_of,), jnp.float32, smallest / len(split), largest / len(split)))
        gain = gain * jnp.repeat(draws, extent[position] // shards_of).reshape([-1 if axis == position else 1 for axis in range(len(extent))])
    return gain


def routed_block(own_key, own, number, rows, amount, top, bound, lean):
    sequence = jax.random.permutation(own_key, amount)
    packed, usual = portions_of(amount, rows * top, bound, lean, True), portions_of(amount, rows * top, bound, lean, False)
    places = jnp.arange(amount)

    def named(tallies, turn):
        used = int((tallies > 0).sum())
        fixed = max(1, used // 4)
        shifted = fixed + (places - fixed + turn * (used - fixed)) % max(1, amount - fixed)
        return jnp.zeros((amount,), jnp.int32).at[sequence[jnp.where(places < fixed, places, shifted)]].set(jnp.asarray(tallies, jnp.int32))

    tallies = jnp.where(number % 4 == 0, named(packed, number // 4), named(usual, number - number // 4 - 1))
    mixed = jax.random.permutation(jax.random.fold_in(own, 3), amount)
    source_of, taker = mixed[0:amount // 2 * 2:2], mixed[1:amount // 2 * 2:2]
    margin = jnp.minimum(tallies[source_of] - 1, bound - tallies[taker]) // 2
    margin = jnp.where((source_of == sequence[0]) | (taker == sequence[0]) | (tallies[taker] == 0), 0, jnp.maximum(margin, 0))
    shifted = jax.random.randint(jax.random.fold_in(own, 4), (amount // 2,), 0, 1 << 20) % (margin + 1)
    tallies = tallies.at[source_of].add(-shifted).at[taker].add(shifted)
    members = jnp.searchsorted(jnp.cumsum(tallies), jnp.arange(rows * top), side="right").astype(jnp.int32)
    listing = members.reshape(top, rows).T
    listing = listing[jax.random.permutation(jax.random.fold_in(own, 1), rows)]
    turn = jax.random.randint(jax.random.fold_in(own, 2), (rows, 1), 0, top)
    return jnp.take_along_axis(listing, (jnp.arange(top)[None, :] + turn) % top, axis=1)


def portions_of(count, total, reach, skew, full):
    loads = [(1 << 20) // math.isqrt(standing ** skew) + 1 for standing in range(1, count + 1)]
    largest = reach if full else min(reach, max(-(-total // count), total * loads[0] // sum(loads)))
    least = 1 if total - largest >= count - 1 else 0
    holding, spare = [largest] + [least] * (count - 1), total - largest - least * (count - 1)
    while spare > 0:
        candidates = [i for i in range(1, count) if holding[i] < largest] or [i for i in range(1, count) if holding[i] < reach]
        mass, left = sum([loads[i] for i in candidates]), spare
        for i in candidates:
            more = min(reach - holding[i], max(1, left * loads[i] // mass), spare)
            holding[i] = holding[i] + more
            spare = spare - more
    return np.array(holding)


def centred(own_key, extent, scale, bound, pieces=(), kind=jnp.bfloat16):
    drawn = scale * jax.random.normal(own_key, extent, jnp.float32)
    if pieces:
        drawn = drawn * levels(own_key, extent, pieces, -0.22, 0.18)
    return jnp.clip(drawn, -bound, bound).astype(kind)


def bell_draw_with(key, extent, scale, limit, cuts, heavy, kind=jnp.bfloat16):
    drawn = scale * jax.random.normal(key, extent, jnp.float32)
    if cuts:
        drawn = drawn * levels(key, extent, cuts, -0.22, 0.18)
    return jnp.clip(spiked(drawn, jax.random.fold_in(key, 3), *heavy), -limit, limit).astype(kind)


def setup_inputs(seed: int = 0) -> dict:
    seeds = jax.random.split(jax.random.key(seed), 12)
    handoff = centred(seeds[0], (SECTIONS, TOKENS, D), 1.0, 6.0, ((0, 4), (1, 8)))
    saved_in = bell_draw_with(seeds[1], (SECTIONS, TOKENS, D), 1.0, 6.0, ((0, 4), (1, 8)), (1, 2, 8, 2.0))
    grad_handoff = centred(seeds[2], (SECTIONS, TOKENS, D), 1.0, 6.0, ((0, 4), (1, 8)))
    route_fwd_keys = jax.random.split(jax.random.fold_in(seeds[3], 1), SECTIONS * TOKENS // TOK_DEV)
    route_fwd_turns = jax.random.permutation(jax.random.fold_in(seeds[3], 3), SECTIONS * TOKENS // TOK_DEV)
    route_fwd = jax.vmap(lambda own, number: routed_block(jax.random.fold_in(seeds[3], 2), own, number, TOK_DEV, EXPERTS, 2, CAP, 2))(route_fwd_keys, route_fwd_turns).reshape((SECTIONS, TOKENS, 2))
    route_bwd_keys = jax.random.split(jax.random.fold_in(seeds[4], 1), SECTIONS * TOKENS // TOK_DEV)
    route_bwd_turns = jax.random.permutation(jax.random.fold_in(seeds[4], 3), SECTIONS * TOKENS // TOK_DEV)
    route_bwd = jax.vmap(lambda own, number: routed_block(jax.random.fold_in(seeds[4], 2), own, number, TOK_DEV, EXPERTS, 2, CAP, 2))(route_bwd_keys, route_bwd_turns).reshape((SECTIONS, TOKENS, 2))
    norm_gain = draw_norm_gain(jax.random.fold_in(seeds[11], 71), 0)
    router = centred(seeds[6], (SECTIONS, D, EXPERTS), D ** -0.5, 0.125, ((0, 4),))
    up_proj = centred(seeds[7], (SECTIONS, D, EXPERTS * FF), D ** -0.5, 0.125, ((0, 4), (2, 8)))
    down_proj = centred(seeds[8], (SECTIONS, EXPERTS * FF, D), FF ** -0.5, 0.25, ((0, 4), (1, 8)))
    moment_m = centred(seeds[9], (SECTIONS, D, EXPERTS), 0.001, 0.006, ((0, 4), (1, 8)), jnp.float32)
    moment_v = jnp.clip(jnp.exp(math.log(3.999999989900971e-06) - 3.6888794 * jax.random.uniform(seeds[10], (SECTIONS, D, EXPERTS), jnp.float32) ** levels(seeds[10], (SECTIONS, D, EXPERTS), ((0, 4), (1, 8)), -0.2, 0.2)), 1.0000000116860974e-07, 3.999999989900971e-06)
    return dict(handoff=handoff, saved_in=saved_in, grad_handoff=grad_handoff, route_fwd=route_fwd, route_bwd=route_bwd, norm_gain=norm_gain, router=router, up_proj=up_proj, down_proj=down_proj, moment_m=moment_m, moment_v=moment_v)


gelu_scale = math.sqrt(2.0 / math.pi)
beta_first = 0.9
beta_second = 0.95
clip_norm = 1.0

def gelu_parts(preact):
    square = preact * preact
    tangent = jnp.tanh(gelu_scale * (preact + 0.044715 * square * preact))
    activated = 0.5 * preact * (1.0 + tangent)
    gelu_slope = 0.5 * (1.0 + tangent) + 0.5 * preact * (1.0 - tangent * tangent) * gelu_scale * (1.0 + 0.134145 * square)
    return (activated, gelu_slope)

def normalize(inputs, gain_row):
    widened = inputs.astype(jnp.float32)
    inv_rms = lax.rsqrt(lax.optimization_barrier(jnp.mean(widened * widened, axis=-1, keepdims=True)) + 1e-05)
    scaled = widened * inv_rms
    return ((scaled * gain_row).astype(jnp.bfloat16), scaled, inv_rms)

def route_gates(normed, router_table, routes):
    logits = jnp.dot(normed, router_table, preferred_element_type=jnp.float32)
    chosen = jnp.take_along_axis(logits, routes, axis=1)
    first_gate = jax.nn.sigmoid(chosen[:, 0] - chosen[:, 1])
    second = jax.nn.sigmoid(chosen[:, 1] - chosen[:, 0])
    return jnp.stack([first_gate, second], axis=1)

def expert_forward(row_block, up_expert, down_expert):
    preact = jnp.dot(row_block, up_expert, preferred_element_type=jnp.float32)
    activated = gelu_parts(preact)[0]
    return jnp.dot(activated.astype(jnp.bfloat16), down_expert, preferred_element_type=jnp.float32).astype(jnp.bfloat16)

def expert_backward(row_block, grad_rows, up_expert, down_expert):
    preact = jnp.dot(row_block, up_expert, preferred_element_type=jnp.float32)
    activated, gelu_slope = gelu_parts(preact)
    outputs = jnp.dot(activated.astype(jnp.bfloat16), down_expert, preferred_element_type=jnp.float32).astype(jnp.bfloat16)
    hidden_grad = jnp.dot(grad_rows, down_expert.T, preferred_element_type=jnp.float32)
    back_pre = (hidden_grad * gelu_slope).astype(jnp.bfloat16)
    input_grads = jnp.dot(back_pre, up_expert.T, preferred_element_type=jnp.float32).astype(jnp.bfloat16)
    return (outputs, input_grads)

def run_section(entering, saved, arriving, routes_fwd, routes_bwd, gain_row, router_table, up_weights, down_weights):
    normed_fwd = normalize(entering, gain_row)[0]
    gates_fwd = route_gates(normed_fwd, router_table, routes_fwd)
    normed_bwd, scaled_bwd, inv_rms = normalize(saved, gain_row)
    gates_bwd = route_gates(normed_bwd, router_table, routes_bwd)
    cotangent = arriving.astype(jnp.float32)
    slot_grads = (gates_bwd[:, :, None] * cotangent[:, None, :]).astype(jnp.bfloat16).reshape(-1, D)
    flat_fwd = routes_fwd.reshape(-1)
    flat_bwd = routes_bwd.reshape(-1)
    sentinel = 2 * TOKENS

    def per_expert(carried, expert):
        acc_fwd, acc_bwd, acc_grad = carried
        up_expert = lax.dynamic_slice_in_dim(up_weights, expert * FF, FF, 1)
        down_expert = lax.dynamic_slice_in_dim(down_weights, expert * FF, FF, 0)
        index_fwd = jnp.nonzero(flat_fwd == expert, size=MOST_ROWS, fill_value=sentinel)[0].astype(jnp.int32)
        rows_fwd = jnp.take(normed_fwd, index_fwd // 2, axis=0, mode='clip')
        acc_fwd = acc_fwd.at[index_fwd].set(expert_forward(rows_fwd, up_expert, down_expert), mode='drop')
        index_bwd = jnp.nonzero(flat_bwd == expert, size=MOST_ROWS, fill_value=sentinel)[0].astype(jnp.int32)
        rows_bwd = jnp.take(normed_bwd, index_bwd // 2, axis=0, mode='clip')
        grad_rows = jnp.take(slot_grads, index_bwd, axis=0, mode='clip')
        out_rows, grad_in = expert_backward(rows_bwd, grad_rows, up_expert, down_expert)
        acc_bwd = acc_bwd.at[index_bwd].set(out_rows, mode='drop')
        acc_grad = acc_grad.at[index_bwd].set(grad_in, mode='drop')
        return ((acc_fwd, acc_bwd, acc_grad), None)
    blank_rows = jnp.zeros((sentinel, D), jnp.bfloat16)
    carried, unused = lax.scan(per_expert, (blank_rows, blank_rows, blank_rows), jnp.arange(EXPERTS, dtype=jnp.int32))
    out_fwd = carried[0].reshape(TOKENS, 2, D).astype(jnp.float32)
    out_bwd = carried[1].reshape(TOKENS, 2, D).astype(jnp.float32)
    grads_in = carried[2].reshape(TOKENS, 2, D).astype(jnp.float32)
    segment_sum = entering.astype(jnp.float32) + gates_fwd[:, 0:1] * out_fwd[:, 0] + gates_fwd[:, 1:2] * out_fwd[:, 1]
    gate_grads = lax.optimization_barrier(jnp.sum(cotangent[:, None, :] * out_bwd, axis=2))
    logit_step = gates_bwd[:, 0] * gates_bwd[:, 1] * (gate_grads[:, 0] - gate_grads[:, 1])
    columns = jnp.arange(EXPERTS, dtype=jnp.int32)[None, :]
    onehot_first = (routes_bwd[:, 0:1] == columns).astype(jnp.float32)
    onehot_second = (routes_bwd[:, 1:2] == columns).astype(jnp.float32)
    logit_grads = (logit_step[:, None] * (onehot_first - onehot_second)).astype(jnp.bfloat16)
    router_grad = jnp.dot(normed_bwd.T, logit_grads, preferred_element_type=jnp.float32)
    router_back = jnp.dot(logit_grads, router_table.T, preferred_element_type=jnp.float32)
    normed_grad = grads_in[:, 0] + grads_in[:, 1] + router_back
    scaled_grad = normed_grad * gain_row
    input_grad = inv_rms * (scaled_grad - scaled_bwd * lax.optimization_barrier(jnp.mean(scaled_grad * scaled_bwd, axis=-1, keepdims=True)))
    grad_back = (cotangent + input_grad).astype(jnp.bfloat16)
    return (segment_sum.astype(jnp.bfloat16), grad_back, router_grad)

def reference(handoff, saved_in, grad_handoff, route_fwd, route_bwd, norm_gain, router, up_proj, down_proj, moment_m, moment_v):
    segments = []
    backs = []
    router_grads = []
    for section in range(SECTIONS):
        result = run_section(handoff[(section - 1) % SECTIONS], saved_in[section], grad_handoff[(section + 1) % SECTIONS], route_fwd[section], route_bwd[section], norm_gain[section], router[section], up_proj[section], down_proj[section])
        segments.append(result[0])
        backs.append(result[1])
        router_grads.append(result[2])
    segment_out = jnp.stack(segments, axis=0)
    grad_back = jnp.stack(backs, axis=0)
    gradient = jnp.stack(router_grads, axis=0)
    norm_sq = jnp.sum(gradient * gradient)
    factor = jnp.minimum(1.0, clip_norm / jnp.sqrt(norm_sq))
    clipped = gradient * factor
    new_m = beta_first * moment_m + (1.0 - beta_first) * clipped
    new_v = beta_second * moment_v + (1.0 - beta_second) * clipped * clipped
    first_fix = 1.0 - beta_first ** STEP
    second_fix = 1.0 - beta_second ** STEP
    router_update = new_m / first_fix / (jnp.sqrt(new_v / second_fix) + 1e-08)
    return (segment_out, grad_back, new_m, new_v, router_update)
```

```python
import math

import jax
import jax.numpy as jnp
from jax import lax
from jax.experimental import pallas as pl
from jax.experimental.pallas import tpu as pltpu
from jax.sharding import PartitionSpec as P

STEP = 10


gelu_scale = math.sqrt(2.0 / math.pi)
beta_first = 0.9
beta_second = 0.95
clip_norm = 1.0


def shifted(x, axis, by):
    length = lax.axis_size(axis)
    return lax.ppermute(x, axis, [(i, (i + by) % length) for i in range(length)])


def from_partner(value, axis, bit):
    mask = 2**bit
    pairs = [(source, source ^ mask) for source in range(lax.axis_size(axis))]
    return lax.ppermute(value, axis, pairs)


def gelu_parts(preact):
    square = preact * preact
    tangent = jnp.tanh(gelu_scale * (preact + 0.044715 * square * preact))
    activated = 0.5 * preact * (1.0 + tangent)
    gelu_slope = 0.5 * (1.0 + tangent) + 0.5 * preact * (1.0 - tangent * tangent) * gelu_scale * (
        1.0 + 0.134145 * square
    )
    return (activated, gelu_slope)


def normalize(inputs, gain_row):
    widened = inputs.astype(jnp.float32)
    inv_rms = lax.rsqrt(jnp.mean(widened * widened, axis=-1, keepdims=True) + 1e-05)
    scaled = widened * inv_rms
    return ((scaled * gain_row).astype(jnp.bfloat16), scaled, inv_rms)


def route_gates(normed, router_table, routes):
    logits = jnp.dot(normed, router_table, preferred_element_type=jnp.float32)
    columns = jnp.arange(router_table.shape[1], dtype=jnp.int32)
    picked = (routes[:, :, None] == columns[None, None, :]).astype(jnp.float32)
    chosen = jnp.sum(logits[:, None, :] * picked, axis=2)
    first_gate = jax.nn.sigmoid(chosen[:, 0] - chosen[:, 1])
    second = jax.nn.sigmoid(chosen[:, 1] - chosen[:, 0])
    return (jnp.stack([first_gate, second], axis=1), picked)


def slot_plan(routes, half_cap, sender):
    flat_routes = routes.reshape(-1)
    rows = jnp.arange(flat_routes.shape[0], dtype=jnp.int32)
    before = (rows[:, None] > rows[None, :]) & (flat_routes[:, None] == flat_routes[None, :])
    position = jnp.sum(before.astype(jnp.int32), axis=1)
    target = 2 * flat_routes + (position + sender) % 2
    return target * half_cap + position // 2


def pack_rows(row_block, slots, slot_total):
    blank_rows = jnp.zeros((slot_total, row_block.shape[1]), row_block.dtype)
    return blank_rows.at[slots].set(row_block)


def transposed(left, right):
    return lax.dot_general(
        left, right, (((1,), (1,)), ((), ())), preferred_element_type=jnp.float32
    )


def expert_forward(pieces, halves):
    own_up, other_up, own_down, other_down = halves
    row_block = pieces.reshape(-1, pieces.shape[-1])
    active_own = gelu_parts(jnp.dot(row_block, own_up, preferred_element_type=jnp.float32))[
        0
    ].astype(jnp.bfloat16)
    active_other = gelu_parts(jnp.dot(row_block, other_up, preferred_element_type=jnp.float32))[
        0
    ].astype(jnp.bfloat16)
    total = jnp.dot(active_own, own_down, preferred_element_type=jnp.float32) + jnp.dot(
        active_other, other_down, preferred_element_type=jnp.float32
    )
    return total.astype(jnp.bfloat16).reshape(pieces.shape)


def expert_backward(pieces, grad_pieces, halves):
    own_up, other_up, own_down, other_down = halves
    row_block = pieces.reshape(-1, pieces.shape[-1])
    grad_rows = grad_pieces.reshape(-1, pieces.shape[-1])
    active_own, slope_own = gelu_parts(
        jnp.dot(row_block, own_up, preferred_element_type=jnp.float32)
    )
    active_other, slope_other = gelu_parts(
        jnp.dot(row_block, other_up, preferred_element_type=jnp.float32)
    )
    total = jnp.dot(
        active_own.astype(jnp.bfloat16), own_down, preferred_element_type=jnp.float32
    ) + jnp.dot(active_other.astype(jnp.bfloat16), other_down, preferred_element_type=jnp.float32)
    back_own = (transposed(grad_rows, own_down) * slope_own).astype(jnp.bfloat16)
    back_other = (transposed(grad_rows, other_down) * slope_other).astype(jnp.bfloat16)
    input_grads = transposed(back_own, own_up) + transposed(back_other, other_up)
    return (
        total.astype(jnp.bfloat16).reshape(pieces.shape),
        input_grads.astype(jnp.bfloat16).reshape(pieces.shape),
    )


def dispatched(
    handoff,
    saved_in,
    grad_handoff,
    route_fwd,
    route_bwd,
    norm_gain,
    router,
    up_proj,
    down_proj,
    moment_m,
    moment_v,
):
    tok_rows = handoff.shape[1]
    feature_dim = handoff.shape[2]
    devices = lax.axis_size("expert")
    experts = devices // 2
    half_cap = max(3, 3 * tok_rows // (2 * experts))
    slot_total = devices * half_cap
    gain_row = norm_gain[0]
    router_table = router[0]
    sender = lax.axis_index("expert")
    entering = shifted(handoff[0], "pipe", 1)
    arriving = shifted(grad_handoff[0], "pipe", -1)
    own_up = up_proj[0]
    own_down = down_proj[0]
    other_up, other_down = from_partner((own_up, own_down), "expert", 0)
    halves = (own_up, other_up, own_down, other_down)
    normed_fwd = normalize(entering, gain_row)[0]
    gates_fwd = route_gates(normed_fwd, router_table, route_fwd[0])[0]
    slots_fwd = slot_plan(route_fwd[0], half_cap, sender)
    send_fwd = pack_rows(jnp.repeat(normed_fwd, 2, axis=0), slots_fwd, slot_total).reshape(
        devices, half_cap, feature_dim
    )
    normed_bwd, scaled_bwd, inv_rms = normalize(saved_in[0], gain_row)
    gates_bwd, picked = route_gates(normed_bwd, router_table, route_bwd[0])
    slots_bwd = slot_plan(route_bwd[0], half_cap, sender)
    send_bwd = pack_rows(jnp.repeat(normed_bwd, 2, axis=0), slots_bwd, slot_total).reshape(
        devices, half_cap, feature_dim
    )
    cotangent = arriving.astype(jnp.float32)
    slot_grads = (
        (gates_bwd[:, :, None] * cotangent[:, None, :])
        .astype(jnp.bfloat16)
        .reshape(-1, feature_dim)
    )
    send_grad = pack_rows(slot_grads, slots_bwd, slot_total).reshape(devices, half_cap, feature_dim)
    back_fwd = lax.all_to_all(
        expert_forward(
            lax.all_to_all(send_fwd, "expert", split_axis=0, concat_axis=0, tiled=True), halves
        ),
        "expert",
        split_axis=0,
        concat_axis=0,
        tiled=True,
    )
    out_second, grad_second = expert_backward(
        lax.all_to_all(send_bwd, "expert", split_axis=0, concat_axis=0, tiled=True),
        lax.all_to_all(send_grad, "expert", split_axis=0, concat_axis=0, tiled=True),
        halves,
    )
    back_bwd = lax.all_to_all(out_second, "expert", split_axis=0, concat_axis=0, tiled=True)
    back_grad = lax.all_to_all(grad_second, "expert", split_axis=0, concat_axis=0, tiled=True)
    out_fwd = (
        back_fwd.reshape(slot_total, feature_dim)[slots_fwd]
        .reshape(tok_rows, 2, feature_dim)
        .astype(jnp.float32)
    )
    segment_sum = (
        entering.astype(jnp.float32)
        + gates_fwd[:, 0:1] * out_fwd[:, 0]
        + gates_fwd[:, 1:2] * out_fwd[:, 1]
    )
    out_bwd = (
        back_bwd.reshape(slot_total, feature_dim)[slots_bwd]
        .reshape(tok_rows, 2, feature_dim)
        .astype(jnp.float32)
    )
    grads_in = (
        back_grad.reshape(slot_total, feature_dim)[slots_bwd]
        .reshape(tok_rows, 2, feature_dim)
        .astype(jnp.float32)
    )
    gate_grads = jnp.sum(cotangent[:, None, :] * out_bwd, axis=2)
    logit_step = gates_bwd[:, 0] * gates_bwd[:, 1] * (gate_grads[:, 0] - gate_grads[:, 1])
    logit_grads = (logit_step[:, None] * (picked[:, 0, :] - picked[:, 1, :])).astype(jnp.bfloat16)
    local_grad = lax.dot_general(
        normed_bwd, logit_grads, (((0,), (0,)), ((), ())), preferred_element_type=jnp.float32
    )
    router_back = transposed(logit_grads, router_table)
    normed_grad = grads_in[:, 0] + grads_in[:, 1] + router_back
    scaled_grad = normed_grad * gain_row
    input_grad = inv_rms * (
        scaled_grad - scaled_bwd * jnp.mean(scaled_grad * scaled_bwd, axis=-1, keepdims=True)
    )
    grad_back = (cotangent + input_grad).astype(jnp.bfloat16)
    row_count = feature_dim // devices
    summed = lax.psum(local_grad, "expert")
    norm_sq = lax.psum(jnp.sum(summed * summed), "pipe")
    grad_rows = lax.dynamic_slice_in_dim(summed, sender * row_count, row_count, 0)
    factor = jnp.minimum(1.0, clip_norm / jnp.sqrt(norm_sq))
    clipped = grad_rows * factor
    new_m = beta_first * moment_m[0] + (1.0 - beta_first) * clipped
    new_v = beta_second * moment_v[0] + (1.0 - beta_second) * clipped * clipped
    first_fix = 1.0 - beta_first**STEP
    second_fix = 1.0 - beta_second**STEP
    router_update = new_m / first_fix / (jnp.sqrt(new_v / second_fix) + 1e-08)
    return (
        segment_sum.astype(jnp.bfloat16)[None],
        grad_back[None],
        new_m[None],
        new_v[None],
        router_update[None],
    )


PIECES = 4
SLOTS = 16
MIB = 2**20


def permuted(value, axes, target):
    sizes = [lax.axis_size(axis) for axis in axes]
    count = math.prod(sizes)
    pairs = []
    for source in range(count):
        place = (source // sizes[-1], source % sizes[-1]) if len(axes) == 2 else (0, source)
        row, column = target(*place)
        pairs.append((source, (row % sizes[0]) * sizes[-1] + column if len(axes) == 2 else column))
    return lax.ppermute(value, axes if len(axes) == 2 else axes[0], pairs)


def normed_rows(block, gain_row):
    widened = block.astype(jnp.float32)
    inv_rms = lax.rsqrt(jnp.mean(widened * widened, axis=-1, keepdims=True) + 1e-05)
    return (widened * inv_rms * gain_row).astype(jnp.bfloat16)


def gates_of(rows, router_rows, routes):
    logits = lax.dot_general(
        rows, router_rows, (((1,), (1,)), ((), ())), preferred_element_type=jnp.float32
    )
    column = lax.broadcasted_iota(jnp.int32, logits.shape, 1)
    first, second = routes[:, 0:1], routes[:, 1:2]
    logit_first = jnp.sum(jnp.where(column == first, logits, 0.0), axis=1, keepdims=True)
    logit_second = jnp.sum(jnp.where(column == second, logits, 0.0), axis=1, keepdims=True)
    gate_first = jax.nn.sigmoid(logit_first - logit_second)
    gate_second = jax.nn.sigmoid(logit_second - logit_first)
    return first, second, gate_first, gate_second


def start_weights(pieces, up_all, down_all, arrived):
    width = up_all.shape[1] // PIECES
    ups, downs = [], []
    for i in range(PIECES):
        part = pl.ds(i * width, width)
        up = pltpu.make_async_copy(pieces[i], up_all.at[:, part], arrived.at[i])
        down = pltpu.make_async_copy(
            pieces[PIECES + i], down_all.at[part, :], arrived.at[PIECES + i]
        )
        ups.append(up)
        downs.append(down)
    for i in range(PIECES):
        ups[i].start()
        downs[i].start()
    return width, ups, downs


def forward_kernel(held, here, there, gain, router_rows, routes, *rest):
    pieces = rest[: 2 * PIECES]
    kept, sent, up_all, down_all, rows, hidden, arrived = rest[2 * PIECES :]
    width, ups, downs = start_weights(pieces, up_all, down_all, arrived)
    tokens = here.shape[0]
    rows[:tokens, :] = normed_rows(here[...], gain[...])
    rows[tokens:, :] = normed_rows(there[...], gain[...])
    first, second, gate_first, gate_second = gates_of(rows[...], router_rows[...], routes[...])
    for i in range(PIECES):
        expert = held[2 * i // PIECES]
        gate = jnp.where(first == expert, gate_first, 0.0) + jnp.where(
            second == expert, gate_second, 0.0
        )
        part = slice(i * width, (i + 1) * width)
        ups[i].wait()
        preact = jnp.dot(rows[...], up_all[:, part], preferred_element_type=jnp.float32)
        hidden[:, part] = (gelu_parts(preact)[0] * gate).astype(jnp.bfloat16)
    for i in range(PIECES):
        downs[i].wait()
    block = 512
    for start in range(0, kept.shape[1], block):
        part = slice(start, start + block)
        total = jnp.dot(hidden[...], down_all[:, part], preferred_element_type=jnp.float32)
        kept[:, part] = here[:, part].astype(jnp.float32) + total[:tokens]
        sent[:, part] = total[tokens:].astype(jnp.bfloat16)


def backward_kernel(held, here, there, grad_here, grad_there, gain, router_rows, routes, *rest):
    pieces = rest[: 2 * PIECES]
    kept, sent, router_grad, up_all, down_all, rows, grads, backs, arrived = rest[2 * PIECES :]
    width, ups, downs = start_weights(pieces, up_all, down_all, arrived)
    tokens = here.shape[0]
    rows[:tokens, :] = normed_rows(here[...], gain[...])
    rows[tokens:, :] = normed_rows(there[...], gain[...])
    grads[:tokens, :] = grad_here[...]
    grads[tokens:, :] = grad_there[...]
    first, second, gate_first, gate_second = gates_of(rows[...], router_rows[...], routes[...])
    signed_sum = jnp.zeros_like(gate_first)
    for i in range(PIECES):
        expert = held[2 * i // PIECES]
        gate = jnp.where(first == expert, gate_first, 0.0) + jnp.where(
            second == expert, gate_second, 0.0
        )
        sign = jnp.where(first == expert, 1.0, 0.0) - jnp.where(second == expert, 1.0, 0.0)
        part = slice(i * width, (i + 1) * width)
        ups[i].wait()
        preact = jnp.dot(rows[...], up_all[:, part], preferred_element_type=jnp.float32)
        downs[i].wait()
        hidden_grad = transposed(grads[...], down_all[part, :])
        active, slope = gelu_parts(preact)
        active = active.astype(jnp.bfloat16).astype(jnp.float32)
        signed_sum += sign * jnp.sum(active * hidden_grad, axis=1, keepdims=True)
        backs[:, part] = (hidden_grad * slope * gate).astype(jnp.bfloat16)
    step = gate_first * gate_second * signed_sum
    column = lax.broadcasted_iota(jnp.int32, (2 * tokens, SLOTS), 1)
    expert = jnp.where(column < SLOTS // 4, column, column - SLOTS // 4)
    step = jnp.where(expert == first, step, 0.0) - jnp.where(expert == second, step, 0.0)
    coarse = step.astype(jnp.bfloat16).astype(jnp.float32)
    logit_grads = jnp.where(column < SLOTS // 4, coarse, step - coarse)
    logit_grads = jnp.where(column < SLOTS // 2, logit_grads, 0.0).astype(jnp.bfloat16)
    block = 512
    for start in range(0, kept.shape[1], block):
        part = slice(start, start + block)
        router_grad[:, part] = lax.dot_general(
            logit_grads,
            rows[:, part],
            (((0,), (0,)), ((), ())),
            preferred_element_type=jnp.float32,
        )
        total = transposed(backs[...], up_all[part, :]) + jnp.dot(
            logit_grads, router_rows[:, part], preferred_element_type=jnp.float32
        )
        kept[:, part] = total[:tokens]
        sent[:, part] = total[tokens:].astype(jnp.bfloat16)


def closing_kernel(saved, arriving, gain, kept, came, out):
    widened = saved[...].astype(jnp.float32)
    inv_rms = lax.rsqrt(jnp.mean(widened * widened, axis=-1, keepdims=True) + 1e-05)
    scaled = widened * inv_rms
    scaled_grad = (kept[...] + came[...].astype(jnp.float32)) * gain[...]
    mean = jnp.mean(scaled_grad * scaled, axis=-1, keepdims=True)
    input_grad = inv_rms * (scaled_grad - scaled * mean)
    out[...] = (arriving[...].astype(jnp.float32) + input_grad).astype(jnp.bfloat16)


def in_vmem(count):
    return [pl.BlockSpec(memory_space=pltpu.VMEM)] * count


def run_forward(held, here, there, gain, router_rows, routes, pieces):
    tokens, features = here.shape
    hidden = PIECES * pieces[0].shape[1]
    return pl.pallas_call(
        forward_kernel,
        out_shape=(
            jax.ShapeDtypeStruct((tokens, features), jnp.float32),
            jax.ShapeDtypeStruct((tokens, features), jnp.bfloat16),
        ),
        in_specs=[pl.BlockSpec(memory_space=pltpu.SMEM)]
        + in_vmem(5)
        + [pl.BlockSpec(memory_space=pl.ANY)] * (2 * PIECES),
        out_specs=tuple(in_vmem(2)),
        scratch_shapes=[
            pltpu.VMEM((features, hidden), jnp.bfloat16),
            pltpu.VMEM((hidden, features), jnp.bfloat16),
            pltpu.VMEM((2 * tokens, features), jnp.bfloat16),
            pltpu.VMEM((2 * tokens, hidden), jnp.bfloat16),
            pltpu.SemaphoreType.DMA((2 * PIECES,)),
        ],
        compiler_params=pltpu.CompilerParams(vmem_limit_bytes=40 * MIB),
        cost_estimate=pl.CostEstimate(
            flops=8 * tokens * features * hidden,
            bytes_accessed=4 * features * hidden + 12 * tokens * features,
            transcendentals=2 * tokens * hidden,
        ),
    )(held, here, there, gain, router_rows, routes, *pieces)


def run_backward(held, here, there, grad_here, grad_there, gain, router_rows, routes, pieces):
    tokens, features = here.shape
    hidden = PIECES * pieces[0].shape[1]
    return pl.pallas_call(
        backward_kernel,
        out_shape=(
            jax.ShapeDtypeStruct((tokens, features), jnp.float32),
            jax.ShapeDtypeStruct((tokens, features), jnp.bfloat16),
            jax.ShapeDtypeStruct((SLOTS, features), jnp.float32),
        ),
        in_specs=[pl.BlockSpec(memory_space=pltpu.SMEM)]
        + in_vmem(7)
        + [pl.BlockSpec(memory_space=pl.ANY)] * (2 * PIECES),
        out_specs=tuple(in_vmem(3)),
        scratch_shapes=[
            pltpu.VMEM((features, hidden), jnp.bfloat16),
            pltpu.VMEM((hidden, features), jnp.bfloat16),
            pltpu.VMEM((2 * tokens, features), jnp.bfloat16),
            pltpu.VMEM((2 * tokens, features), jnp.bfloat16),
            pltpu.VMEM((2 * tokens, hidden), jnp.bfloat16),
            pltpu.SemaphoreType.DMA((2 * PIECES,)),
        ],
        compiler_params=pltpu.CompilerParams(vmem_limit_bytes=40 * MIB),
        cost_estimate=pl.CostEstimate(
            flops=12 * tokens * features * hidden,
            bytes_accessed=4 * features * hidden + 16 * tokens * features,
            transcendentals=2 * tokens * hidden,
        ),
    )(held, here, there, grad_here, grad_there, gain, router_rows, routes, *pieces)


def run_closing(saved, arriving, gain, kept, came):
    tokens, features = saved.shape
    block = tokens // 4
    rows = pl.BlockSpec((block, features), lambda i: (i, 0))
    return pl.pallas_call(
        closing_kernel,
        out_shape=jax.ShapeDtypeStruct((tokens, features), jnp.bfloat16),
        grid=(4,),
        in_specs=[rows, rows, pl.BlockSpec((1, features), lambda i: (0, 0)), rows, rows],
        out_specs=rows,
        cost_estimate=pl.CostEstimate(
            flops=16 * tokens * features, bytes_accessed=12 * tokens * features, transcendentals=0
        ),
    )(saved, arriving, gain, kept, came)


def paired(
    handoff,
    saved_in,
    grad_handoff,
    route_fwd,
    route_bwd,
    norm_gain,
    router,
    up_proj,
    down_proj,
    moment_m,
    moment_v,
):
    def mirror(place):
        return place ^ 6

    both, line = ("pipe", "expert"), ("expert",)
    sender = lax.axis_index("expert")
    own_up, own_down = up_proj[0], down_proj[0]
    near_up = permuted(own_up, line, lambda row, place: (row, place ^ 2))
    near_down = permuted(own_down, line, lambda row, place: (row, place ^ 2))
    entering_there = permuted(handoff[0], both, lambda row, place: (row + 1, mirror(place)))
    entering = permuted(handoff[0], both, lambda row, place: (row + 1, place))
    own_up_other, own_down_other = permuted(
        (own_up, own_down), line, lambda row, place: (row, place ^ 1)
    )
    routes = jnp.concatenate([route_fwd[0].T, route_bwd[0].T], axis=0)
    routes_there = permuted(routes, line, lambda row, place: (row, mirror(place)))
    saved = saved_in[0]
    saved_there = permuted(saved, line, lambda row, place: (row, mirror(place)))
    arriving_there = permuted(grad_handoff[0], both, lambda row, place: (row - 1, mirror(place)))
    arriving = permuted(grad_handoff[0], both, lambda row, place: (row - 1, place))
    near_up_other, near_down_other = permuted(
        (near_up, near_down), line, lambda row, place: (row, place ^ 1)
    )
    pieces = (
        own_up,
        own_up_other,
        near_up,
        near_up_other,
        own_down,
        own_down_other,
        near_down,
        near_down_other,
    )
    all_routes = jnp.concatenate([routes, routes_there], axis=1)
    routes_fwd, routes_bwd = all_routes[:2].T, all_routes[2:].T
    chip = sender // 2
    held = jnp.stack([chip, chip ^ 1]).astype(jnp.int32)
    router_turned = router[0].T
    router_rows = jnp.concatenate(
        [router_turned, router_turned, jnp.zeros((SLOTS // 2, router_turned.shape[1]), jnp.bfloat16)]
    )
    kept_fwd, sent_fwd = run_forward(
        held, entering, entering_there, norm_gain, router_rows, routes_fwd, pieces
    )
    came_fwd = permuted(sent_fwd, line, lambda row, place: (row, mirror(place)))
    kept_bwd, sent_bwd, router_parts = run_backward(
        held,
        saved,
        saved_there,
        arriving,
        arriving_there,
        norm_gain,
        router_rows,
        routes_bwd,
        pieces,
    )
    came_bwd = permuted(sent_bwd, line, lambda row, place: (row, mirror(place)))
    segment_out = (kept_fwd + came_fwd.astype(jnp.float32)).astype(jnp.bfloat16)
    grad_back = run_closing(saved, arriving, norm_gain, kept_bwd, came_bwd)
    quarter = SLOTS // 4
    local_grad = router_parts[:quarter] + router_parts[quarter : 2 * quarter]
    grad_rows = lax.psum_scatter(local_grad, "expert", scatter_dimension=1, tiled=True)
    norm_sq = lax.psum(jnp.sum(grad_rows * grad_rows), both)
    factor = jnp.minimum(1.0, clip_norm / jnp.sqrt(norm_sq))
    clipped = grad_rows.T * factor
    new_m = beta_first * moment_m[0] + (1.0 - beta_first) * clipped
    new_v = beta_second * moment_v[0] + (1.0 - beta_second) * clipped * clipped
    first_fix = 1.0 - beta_first**STEP
    second_fix = 1.0 - beta_second**STEP
    router_update = new_m / first_fix / (jnp.sqrt(new_v / second_fix) + 1e-08)
    return (
        segment_out[None],
        grad_back[None],
        new_m[None],
        new_v[None],
        router_update[None],
    )


def solution(mesh):
    in_specs = (
        P("pipe", "expert", None),
        P("pipe", "expert", None),
        P("pipe", "expert", None),
        P("pipe", "expert", None),
        P("pipe", "expert", None),
        P("pipe", None),
        P("pipe", None, None),
        P("pipe", None, "expert"),
        P("pipe", "expert", None),
        P("pipe", "expert", None),
        P("pipe", "expert", None),
    )
    out_specs = (
        P("pipe", "expert", None),
        P("pipe", "expert", None),
        P("pipe", "expert", None),
        P("pipe", "expert", None),
        P("pipe", "expert", None),
    )
    experts_held = mesh.shape["expert"] // 2
    return jax.shard_map(
        paired if experts_held == 4 else dispatched, mesh=mesh, in_specs=in_specs, out_specs=out_specs, check_vma=False
    )
```

```python
import math

import jax
import jax.numpy as jnp
from jax import lax
from jax.experimental import pallas as pl
from jax.experimental.pallas import tpu as pltpu
from jax.sharding import PartitionSpec as P

STEP = 10


gelu_scale = math.sqrt(2.0 / math.pi)
beta_first = 0.9
beta_second = 0.95
clip_norm = 1.0


def shifted(x, axis, by):
    length = lax.axis_size(axis)
    return lax.ppermute(x, axis, [(i, (i + by) % length) for i in range(length)])


def from_partner(value, axis, bit):
    mask = 2**bit
    pairs = [(source, source ^ mask) for source in range(lax.axis_size(axis))]
    return lax.ppermute(value, axis, pairs)


def gelu_parts(preact):
    square = preact * preact
    tangent = jnp.tanh(gelu_scale * (preact + 0.044715 * square * preact))
    activated = 0.5 * preact * (1.0 + tangent)
    gelu_slope = 0.5 * (1.0 + tangent) + 0.5 * preact * (1.0 - tangent * tangent) * gelu_scale * (
        1.0 + 0.134145 * square
    )
    return (activated, gelu_slope)


def normalize(inputs, gain_row):
    widened = inputs.astype(jnp.float32)
    inv_rms = lax.rsqrt(jnp.mean(widened * widened, axis=-1, keepdims=True) + 1e-05)
    scaled = widened * inv_rms
    return ((scaled * gain_row).astype(jnp.bfloat16), scaled, inv_rms)


def route_gates(normed, router_table, routes):
    logits = jnp.dot(normed, router_table, preferred_element_type=jnp.float32)
    columns = jnp.arange(router_table.shape[1], dtype=jnp.int32)
    picked = (routes[:, :, None] == columns[None, None, :]).astype(jnp.float32)
    chosen = jnp.sum(logits[:, None, :] * picked, axis=2)
    first_gate = jax.nn.sigmoid(chosen[:, 0] - chosen[:, 1])
    second = jax.nn.sigmoid(chosen[:, 1] - chosen[:, 0])
    return (jnp.stack([first_gate, second], axis=1), picked)


def slot_plan(routes, half_cap, sender):
    flat_routes = routes.reshape(-1)
    rows = jnp.arange(flat_routes.shape[0], dtype=jnp.int32)
    before = (rows[:, None] > rows[None, :]) & (flat_routes[:, None] == flat_routes[None, :])
    position = jnp.sum(before.astype(jnp.int32), axis=1)
    target = 2 * flat_routes + (position + sender) % 2
    return target * half_cap + position // 2


def pack_rows(row_block, slots, slot_total):
    blank_rows = jnp.zeros((slot_total, row_block.shape[1]), row_block.dtype)
    return blank_rows.at[slots].set(row_block)


def transposed(left, right):
    return lax.dot_general(
        left, right, (((1,), (1,)), ((), ())), preferred_element_type=jnp.float32
    )


def expert_forward(pieces, halves):
    own_up, other_up, own_down, other_down = halves
    row_block = pieces.reshape(-1, pieces.shape[-1])
    active_own = gelu_parts(jnp.dot(row_block, own_up, preferred_element_type=jnp.float32))[
        0
    ].astype(jnp.bfloat16)
    active_other = gelu_parts(jnp.dot(row_block, other_up, preferred_element_type=jnp.float32))[
        0
    ].astype(jnp.bfloat16)
    total = jnp.dot(active_own, own_down, preferred_element_type=jnp.float32) + jnp.dot(
        active_other, other_down, preferred_element_type=jnp.float32
    )
    return total.astype(jnp.bfloat16).reshape(pieces.shape)


def expert_backward(pieces, grad_pieces, halves):
    own_up, other_up, own_down, other_down = halves
    row_block = pieces.reshape(-1, pieces.shape[-1])
    grad_rows = grad_pieces.reshape(-1, pieces.shape[-1])
    active_own, slope_own = gelu_parts(
        jnp.dot(row_block, own_up, preferred_element_type=jnp.float32)
    )
    active_other, slope_other = gelu_parts(
        jnp.dot(row_block, other_up, preferred_element_type=jnp.float32)
    )
    total = jnp.dot(
        active_own.astype(jnp.bfloat16), own_down, preferred_element_type=jnp.float32
    ) + jnp.dot(active_other.astype(jnp.bfloat16), other_down, preferred_element_type=jnp.float32)
    back_own = (transposed(grad_rows, own_down) * slope_own).astype(jnp.bfloat16)
    back_other = (transposed(grad_rows, other_down) * slope_other).astype(jnp.bfloat16)
    input_grads = transposed(back_own, own_up) + transposed(back_other, other_up)
    return (
        total.astype(jnp.bfloat16).reshape(pieces.shape),
        input_grads.astype(jnp.bfloat16).reshape(pieces.shape),
    )


def dispatched(
    handoff,
    saved_in,
    grad_handoff,
    route_fwd,
    route_bwd,
    norm_gain,
    router,
    up_proj,
    down_proj,
    moment_m,
    moment_v,
):
    tok_rows = handoff.shape[1]
    feature_dim = handoff.shape[2]
    devices = lax.axis_size("expert")
    experts = devices // 2
    half_cap = max(3, 3 * tok_rows // (2 * experts))
    slot_total = devices * half_cap
    gain_row = norm_gain[0]
    router_table = router[0]
    sender = lax.axis_index("expert")
    entering = shifted(handoff[0], "pipe", 1)
    arriving = shifted(grad_handoff[0], "pipe", -1)
    own_up = up_proj[0]
    own_down = down_proj[0]
    other_up, other_down = from_partner((own_up, own_down), "expert", 0)
    halves = (own_up, other_up, own_down, other_down)
    normed_fwd = normalize(entering, gain_row)[0]
    gates_fwd = route_gates(normed_fwd, router_table, route_fwd[0])[0]
    slots_fwd = slot_plan(route_fwd[0], half_cap, sender)
    send_fwd = pack_rows(jnp.repeat(normed_fwd, 2, axis=0), slots_fwd, slot_total).reshape(
        devices, half_cap, feature_dim
    )
    normed_bwd, scaled_bwd, inv_rms = normalize(saved_in[0], gain_row)
    gates_bwd, picked = route_gates(normed_bwd, router_table, route_bwd[0])
    slots_bwd = slot_plan(route_bwd[0], half_cap, sender)
    send_bwd = pack_rows(jnp.repeat(normed_bwd, 2, axis=0), slots_bwd, slot_total).reshape(
        devices, half_cap, feature_dim
    )
    cotangent = arriving.astype(jnp.float32)
    slot_grads = (
        (gates_bwd[:, :, None] * cotangent[:, None, :])
        .astype(jnp.bfloat16)
        .reshape(-1, feature_dim)
    )
    send_grad = pack_rows(slot_grads, slots_bwd, slot_total).reshape(devices, half_cap, feature_dim)
    back_fwd = lax.all_to_all(
        expert_forward(
            lax.all_to_all(send_fwd, "expert", split_axis=0, concat_axis=0, tiled=True), halves
        ),
        "expert",
        split_axis=0,
        concat_axis=0,
        tiled=True,
    )
    out_second, grad_second = expert_backward(
        lax.all_to_all(send_bwd, "expert", split_axis=0, concat_axis=0, tiled=True),
        lax.all_to_all(send_grad, "expert", split_axis=0, concat_axis=0, tiled=True),
        halves,
    )
    back_bwd = lax.all_to_all(out_second, "expert", split_axis=0, concat_axis=0, tiled=True)
    back_grad = lax.all_to_all(grad_second, "expert", split_axis=0, concat_axis=0, tiled=True)
    out_fwd = (
        back_fwd.reshape(slot_total, feature_dim)[slots_fwd]
        .reshape(tok_rows, 2, feature_dim)
        .astype(jnp.float32)
    )
    segment_sum = (
        entering.astype(jnp.float32)
        + gates_fwd[:, 0:1] * out_fwd[:, 0]
        + gates_fwd[:, 1:2] * out_fwd[:, 1]
    )
    out_bwd = (
        back_bwd.reshape(slot_total, feature_dim)[slots_bwd]
        .reshape(tok_rows, 2, feature_dim)
        .astype(jnp.float32)
    )
    grads_in = (
        back_grad.reshape(slot_total, feature_dim)[slots_bwd]
        .reshape(tok_rows, 2, feature_dim)
        .astype(jnp.float32)
    )
    gate_grads = jnp.sum(cotangent[:, None, :] * out_bwd, axis=2)
    logit_step = gates_bwd[:, 0] * gates_bwd[:, 1] * (gate_grads[:, 0] - gate_grads[:, 1])
    logit_grads = (logit_step[:, None] * (picked[:, 0, :] - picked[:, 1, :])).astype(jnp.bfloat16)
    local_grad = lax.dot_general(
        normed_bwd, logit_grads, (((0,), (0,)), ((), ())), preferred_element_type=jnp.float32
    )
    router_back = transposed(logit_grads, router_table)
    normed_grad = grads_in[:, 0] + grads_in[:, 1] + router_back
    scaled_grad = normed_grad * gain_row
    input_grad = inv_rms * (
        scaled_grad - scaled_bwd * jnp.mean(scaled_grad * scaled_bwd, axis=-1, keepdims=True)
    )
    grad_back = (cotangent + input_grad).astype(jnp.bfloat16)
    row_count = feature_dim // devices
    summed = lax.psum(local_grad, "expert")
    norm_sq = lax.psum(jnp.sum(summed * summed), "pipe")
    grad_rows = lax.dynamic_slice_in_dim(summed, sender * row_count, row_count, 0)
    factor = jnp.minimum(1.0, clip_norm / jnp.sqrt(norm_sq))
    clipped = grad_rows * factor
    new_m = beta_first * moment_m[0] + (1.0 - beta_first) * clipped
    new_v = beta_second * moment_v[0] + (1.0 - beta_second) * clipped * clipped
    first_fix = 1.0 - beta_first**STEP
    second_fix = 1.0 - beta_second**STEP
    router_update = new_m / first_fix / (jnp.sqrt(new_v / second_fix) + 1e-08)
    return (
        segment_sum.astype(jnp.bfloat16)[None],
        grad_back[None],
        new_m[None],
        new_v[None],
        router_update[None],
    )


PIECES = 4
SLOTS = 16
MIB = 2**20


def permuted(value, axes, target):
    sizes = [lax.axis_size(axis) for axis in axes]
    count = math.prod(sizes)
    pairs = []
    for source in range(count):
        place = (source // sizes[-1], source % sizes[-1]) if len(axes) == 2 else (0, source)
        row, column = target(*place)
        pairs.append((source, (row % sizes[0]) * sizes[-1] + column if len(axes) == 2 else column))
    return lax.ppermute(value, axes if len(axes) == 2 else axes[0], pairs)


def normed_rows(block, gain_row):
    widened = block.astype(jnp.float32)
    inv_rms = lax.rsqrt(jnp.mean(widened * widened, axis=-1, keepdims=True) + 1e-05)
    return (widened * inv_rms * gain_row).astype(jnp.bfloat16)


def gates_of(rows, router_rows, routes):
    logits = lax.dot_general(
        rows, router_rows, (((1,), (1,)), ((), ())), preferred_element_type=jnp.float32
    )
    column = lax.broadcasted_iota(jnp.int32, logits.shape, 1)
    first, second = routes[:, 0:1], routes[:, 1:2]
    logit_first = jnp.sum(jnp.where(column == first, logits, 0.0), axis=1, keepdims=True)
    logit_second = jnp.sum(jnp.where(column == second, logits, 0.0), axis=1, keepdims=True)
    gate_first = jax.nn.sigmoid(logit_first - logit_second)
    gate_second = jax.nn.sigmoid(logit_second - logit_first)
    return first, second, gate_first, gate_second


def start_weights(pieces, up_all, down_all, arrived):
    width = up_all.shape[0] // PIECES
    ups, downs = [], []
    for i in range(PIECES):
        part = pl.ds(i * width, width)
        ups.append(
            pltpu.make_async_copy(pieces[i].at[pl.ds(0, width)], up_all.at[part], arrived.at[i])
        )
        downs.append(
            pltpu.make_async_copy(
                pieces[i].at[pl.ds(width, width)], down_all.at[part], arrived.at[PIECES + i]
            )
        )
    for i in range(PIECES):
        ups[i].start()
        downs[i].start()
    return width, ups, downs


def pick(first, second, for_first, for_second, expert):
    return jnp.where(first == expert, for_first, 0.0) + jnp.where(
        second == expert, for_second, 0.0
    )


def expert_kernel(
    held,
    next_here,
    next_there,
    saved_here,
    saved_there,
    grad_here,
    grad_there,
    gain,
    router_rows,
    routes_fwd,
    routes_bwd,
    *rest,
):
    pieces = rest[:PIECES]
    (
        kept_fwd,
        kept_bwd,
        sent,
        router_grad,
        up_all,
        down_all,
        entered,
        saved,
        grads,
        rows_fwd,
        rows_bwd,
        hidden,
        backs,
        arrived,
        landed,
    ) = rest[PIECES:]
    tokens = next_here.shape[0]
    upper, lower = pl.ds(0, tokens), pl.ds(tokens, tokens)
    loads = [
        pltpu.make_async_copy(next_here, entered.at[upper], landed.at[0]),
        pltpu.make_async_copy(next_there, entered.at[lower], landed.at[1]),
        pltpu.make_async_copy(saved_here, saved.at[upper], landed.at[2]),
        pltpu.make_async_copy(saved_there, saved.at[lower], landed.at[3]),
        pltpu.make_async_copy(grad_here, grads.at[upper], landed.at[4]),
        pltpu.make_async_copy(grad_there, grads.at[lower], landed.at[5]),
    ]
    for load in loads:
        load.start()
    width, ups, downs = start_weights(pieces, up_all, down_all, arrived)
    for load in loads[:2]:
        load.wait()
    rows_fwd[...] = normed_rows(entered[...], gain[...])
    for load in loads[2:]:
        load.wait()
    rows_bwd[...] = normed_rows(saved[...], gain[...])
    first_fwd, second_fwd, gate_first_fwd, gate_second_fwd = gates_of(
        rows_fwd[...], router_rows[...], routes_fwd[...]
    )
    first, second, gate_first, gate_second = gates_of(
        rows_bwd[...], router_rows[...], routes_bwd[...]
    )
    signed_sum = jnp.zeros_like(gate_first)
    for i in range(PIECES):
        expert = held[2 * i // PIECES]
        part = slice(i * width, (i + 1) * width)
        ups[i].wait()
        preact = transposed(rows_fwd[...], up_all[part, :])
        gate = pick(first_fwd, second_fwd, gate_first_fwd, gate_second_fwd, expert)
        hidden[:, part] = (gelu_parts(preact)[0] * gate).astype(jnp.bfloat16)
        preact = transposed(rows_bwd[...], up_all[part, :])
        downs[i].wait()
        hidden_grad = transposed(grads[...], down_all[part, :])
        active, slope = gelu_parts(preact)
        active = active.astype(jnp.bfloat16).astype(jnp.float32)
        signed_sum += pick(first, second, 1.0, -1.0, expert) * jnp.sum(
            active * hidden_grad, axis=1, keepdims=True
        )
        gate = pick(first, second, gate_first, gate_second, expert)
        backs[:, part] = (hidden_grad * slope * gate).astype(jnp.bfloat16)
    step = gate_first * gate_second * signed_sum
    column = lax.broadcasted_iota(jnp.int32, (2 * tokens, SLOTS), 1)
    expert = jnp.where(column < SLOTS // 4, column, column - SLOTS // 4)
    step = pick(first, second, step, -step, expert)
    coarse = step.astype(jnp.bfloat16).astype(jnp.float32)
    logit_grads = jnp.where(column < SLOTS // 4, coarse, step - coarse)
    logit_grads = jnp.where(column < SLOTS // 2, logit_grads, 0.0).astype(jnp.bfloat16)
    block = 512
    for start in range(0, kept_bwd.shape[1], block):
        part = slice(start, start + block)
        total = jnp.dot(hidden[...], down_all[:, part], preferred_element_type=jnp.float32)
        kept_fwd[:, part] = entered[:tokens, part].astype(jnp.float32) + total[:tokens]
        sent[:tokens, part] = total[tokens:].astype(jnp.bfloat16)
        router_grad[:, part] = lax.dot_general(
            logit_grads,
            rows_bwd[:, part],
            (((0,), (0,)), ((), ())),
            preferred_element_type=jnp.float32,
        )
        total = jnp.dot(
            backs[...], up_all[:, part], preferred_element_type=jnp.float32
        ) + jnp.dot(logit_grads, router_rows[:, part], preferred_element_type=jnp.float32)
        kept_bwd[:, part] = total[:tokens]
        sent[tokens:, part] = total[tokens:].astype(jnp.bfloat16)


def closing_kernel(saved, arriving, gain, kept, came, out):
    widened = saved[...].astype(jnp.float32)
    inv_rms = lax.rsqrt(jnp.mean(widened * widened, axis=-1, keepdims=True) + 1e-05)
    scaled = widened * inv_rms
    scaled_grad = (kept[...] + came[...].astype(jnp.float32)) * gain[...]
    mean = jnp.mean(scaled_grad * scaled, axis=-1, keepdims=True)
    input_grad = inv_rms * (scaled_grad - scaled * mean)
    out[...] = (arriving[...].astype(jnp.float32) + input_grad).astype(jnp.bfloat16)


def in_hbm(count):
    return [pl.BlockSpec(memory_space=pltpu.HBM)] * count


def in_vmem(count):
    return [pl.BlockSpec(memory_space=pltpu.VMEM)] * count


def run_experts(held, blocks, gain, router_rows, routes, pieces):
    tokens, features = blocks[0].shape
    hidden = PIECES * pieces[0].shape[0] // 2
    kept = jax.ShapeDtypeStruct((tokens, features), jnp.float32)
    sent = jax.ShapeDtypeStruct((2 * tokens, features), jnp.bfloat16)
    rows = pltpu.VMEM((2 * tokens, features), jnp.bfloat16)
    return pl.pallas_call(
        expert_kernel,
        out_shape=(kept, kept, sent, jax.ShapeDtypeStruct((SLOTS, features), jnp.float32)),
        in_specs=[pl.BlockSpec(memory_space=pltpu.SMEM)]
        + in_hbm(6)
        + in_vmem(4)
        + in_hbm(PIECES),
        out_specs=tuple(in_vmem(4)),
        scratch_shapes=[
            pltpu.VMEM((hidden, features), jnp.bfloat16),
            pltpu.VMEM((hidden, features), jnp.bfloat16),
            rows,
            rows,
            rows,
            rows,
            rows,
            pltpu.VMEM((2 * tokens, hidden), jnp.bfloat16),
            pltpu.VMEM((2 * tokens, hidden), jnp.bfloat16),
            pltpu.SemaphoreType.DMA((2 * PIECES,)),
            pltpu.SemaphoreType.DMA((6,)),
        ],
        compiler_params=pltpu.CompilerParams(vmem_limit_bytes=60 * MIB),
        cost_estimate=pl.CostEstimate(
            flops=20 * tokens * features * hidden,
            bytes_accessed=4 * features * hidden + 24 * tokens * features,
            transcendentals=4 * tokens * hidden,
        ),
    )(held, *blocks, gain, router_rows, *routes, *pieces)


def run_closing(saved, arriving, gain, kept, came):
    tokens, features = saved.shape
    block = tokens // 4
    rows = pl.BlockSpec((block, features), lambda i: (i, 0))
    return pl.pallas_call(
        closing_kernel,
        out_shape=jax.ShapeDtypeStruct((tokens, features), jnp.bfloat16),
        grid=(4,),
        in_specs=[
            rows,
            rows,
            pl.BlockSpec((1, features), lambda i: (0, 0)),
            rows,
            pl.BlockSpec((block, features), lambda i: (i + 4, 0)),
        ],
        out_specs=rows,
        cost_estimate=pl.CostEstimate(
            flops=16 * tokens * features, bytes_accessed=12 * tokens * features, transcendentals=0
        ),
    )(saved, arriving, gain, kept, came)


def after(value, *earlier):
    return lax.optimization_barrier((value, *earlier))[0]


def paired(
    handoff,
    saved_in,
    grad_handoff,
    route_fwd,
    route_bwd,
    norm_gain,
    router,
    up_proj,
    down_proj,
    moment_m,
    moment_v,
):
    def shift(value, by):
        return permuted(value, both, lambda row, place: (row + by, place))

    def mirror(value, by=0):
        if by == 0:
            return permuted(value, line, lambda row, place: (row, place ^ 6))
        return permuted(value, both, lambda row, place: (row + by, place ^ 6))

    def near(value):
        return permuted(value, line, lambda row, place: (row, place ^ 2))

    def across(value):
        return permuted(value, line, lambda row, place: (row, place ^ 1))

    both, line = ("pipe", "expert"), ("expert",)
    sender = lax.axis_index("expert")
    saved, leaving, cotangent = saved_in[0], handoff[0], grad_handoff[0]
    routes = jnp.concatenate([route_fwd[0].T, route_bwd[0].T], axis=0)
    routes_there = mirror(routes)
    own = after(jnp.concatenate([up_proj[0].T, down_proj[0]], axis=0), routes_there)
    close = near(own)
    own_other = across(own)
    saved_there = mirror(saved)
    entering = shift(leaving, 1)
    arriving = shift(cotangent, -1)
    entering_there = mirror(after(entering, saved_there, own_other, arriving))
    arriving_there = mirror(after(arriving, saved_there, own_other, entering))
    close_other = across(after(close, arriving_there, entering_there))
    all_routes = jnp.concatenate([routes, routes_there], axis=1)
    chip = sender // 2
    held = jnp.stack([chip, chip ^ 1]).astype(jnp.int32)
    router_turned = router[0].T
    router_rows = jnp.concatenate(
        [router_turned, router_turned, jnp.zeros((SLOTS // 2, router_turned.shape[1]), jnp.bfloat16)]
    )
    kept_fwd, kept_bwd, sent, router_parts = run_experts(
        held,
        (entering, entering_there, saved, saved_there, arriving, arriving_there),
        norm_gain,
        router_rows,
        (all_routes[:2].T, all_routes[2:].T),
        (own, own_other, close, close_other),
    )
    came = mirror(sent)
    quarter = SLOTS // 4
    summed = router_parts[:quarter] + router_parts[quarter : 2 * quarter]
    devices = lax.axis_size("expert")
    sliced = jnp.transpose(summed.reshape(quarter, devices, -1), (1, 0, 2))
    sliced = lax.all_to_all(sliced, "expert", split_axis=0, concat_axis=0, tiled=True)
    grad_rows = jnp.sum(sliced, axis=0)
    ranks = devices * lax.axis_size("pipe")
    square = jnp.broadcast_to(jnp.sum(grad_rows * grad_rows), (ranks, 128))
    norm_sq = jnp.sum(lax.all_to_all(square, both, split_axis=0, concat_axis=0, tiled=True)[:, 0])
    grad_rows = grad_rows.T
    factor = jnp.minimum(1.0, clip_norm / jnp.sqrt(norm_sq))
    clipped = grad_rows * factor
    new_m = beta_first * moment_m[0] + (1.0 - beta_first) * clipped
    new_v = beta_second * moment_v[0] + (1.0 - beta_second) * clipped * clipped
    first_fix = 1.0 - beta_first**STEP
    second_fix = 1.0 - beta_second**STEP
    router_update = new_m / first_fix / (jnp.sqrt(new_v / second_fix) + 1e-08)
    grad_back = run_closing(saved, arriving, norm_gain, kept_bwd, came)
    segment_out = (kept_fwd + came[: kept_fwd.shape[0]].astype(jnp.float32)).astype(jnp.bfloat16)
    return (
        segment_out[None],
        grad_back[None],
        new_m[None],
        new_v[None],
        router_update[None],
    )


def solution(mesh):
    in_specs = (
        P("pipe", "expert", None),
        P("pipe", "expert", None),
        P("pipe", "expert", None),
        P("pipe", "expert", None),
        P("pipe", "expert", None),
        P("pipe", None),
        P("pipe", None, None),
        P("pipe", None, "expert"),
        P("pipe", "expert", None),
        P("pipe", "expert", None),
        P("pipe", "expert", None),
    )
    out_specs = (
        P("pipe", "expert", None),
        P("pipe", "expert", None),
        P("pipe", "expert", None),
        P("pipe", "expert", None),
        P("pipe", "expert", None),
    )
    experts_held = mesh.shape["expert"] // 2
    return jax.shard_map(
        paired if experts_held == 4 else dispatched, mesh=mesh, in_specs=in_specs, out_specs=out_specs, check_vma=False
    )
```

```python
import math

import jax
import jax.numpy as jnp
from jax import lax
from jax.experimental import pallas as pl
from jax.experimental.pallas import tpu as pltpu
from jax.sharding import PartitionSpec as P

STEP = 10


gelu_scale = math.sqrt(2.0 / math.pi)
beta_first = 0.9
beta_second = 0.95
clip_norm = 1.0


def shifted(x, axis, by):
    length = lax.axis_size(axis)
    return lax.ppermute(x, axis, [(i, (i + by) % length) for i in range(length)])


def from_partner(value, axis, bit):
    mask = 2**bit
    pairs = [(source, source ^ mask) for source in range(lax.axis_size(axis))]
    return lax.ppermute(value, axis, pairs)


def gelu_parts(preact):
    square = preact * preact
    tangent = jnp.tanh(gelu_scale * (preact + 0.044715 * square * preact))
    activated = 0.5 * preact * (1.0 + tangent)
    gelu_slope = 0.5 * (1.0 + tangent) + 0.5 * preact * (1.0 - tangent * tangent) * gelu_scale * (
        1.0 + 0.134145 * square
    )
    return (activated, gelu_slope)


def normalize(inputs, gain_row):
    widened = inputs.astype(jnp.float32)
    inv_rms = lax.rsqrt(jnp.mean(widened * widened, axis=-1, keepdims=True) + 1e-05)
    scaled = widened * inv_rms
    return ((scaled * gain_row).astype(jnp.bfloat16), scaled, inv_rms)


def route_gates(normed, router_table, routes):
    logits = jnp.dot(normed, router_table, preferred_element_type=jnp.float32)
    columns = jnp.arange(router_table.shape[1], dtype=jnp.int32)
    picked = (routes[:, :, None] == columns[None, None, :]).astype(jnp.float32)
    chosen = jnp.sum(logits[:, None, :] * picked, axis=2)
    first_gate = jax.nn.sigmoid(chosen[:, 0] - chosen[:, 1])
    second = jax.nn.sigmoid(chosen[:, 1] - chosen[:, 0])
    return (jnp.stack([first_gate, second], axis=1), picked)


def slot_plan(routes, half_cap, sender):
    flat_routes = routes.reshape(-1)
    rows = jnp.arange(flat_routes.shape[0], dtype=jnp.int32)
    before = (rows[:, None] > rows[None, :]) & (flat_routes[:, None] == flat_routes[None, :])
    position = jnp.sum(before.astype(jnp.int32), axis=1)
    target = 2 * flat_routes + (position + sender) % 2
    return target * half_cap + position // 2


def pack_rows(row_block, slots, slot_total):
    blank_rows = jnp.zeros((slot_total, row_block.shape[1]), row_block.dtype)
    return blank_rows.at[slots].set(row_block)


def transposed(left, right):
    return lax.dot_general(
        left, right, (((1,), (1,)), ((), ())), preferred_element_type=jnp.float32
    )


def expert_forward(pieces, halves):
    own_up, other_up, own_down, other_down = halves
    row_block = pieces.reshape(-1, pieces.shape[-1])
    active_own = gelu_parts(jnp.dot(row_block, own_up, preferred_element_type=jnp.float32))[
        0
    ].astype(jnp.bfloat16)
    active_other = gelu_parts(jnp.dot(row_block, other_up, preferred_element_type=jnp.float32))[
        0
    ].astype(jnp.bfloat16)
    total = jnp.dot(active_own, own_down, preferred_element_type=jnp.float32) + jnp.dot(
        active_other, other_down, preferred_element_type=jnp.float32
    )
    return total.astype(jnp.bfloat16).reshape(pieces.shape)


def expert_backward(pieces, grad_pieces, halves):
    own_up, other_up, own_down, other_down = halves
    row_block = pieces.reshape(-1, pieces.shape[-1])
    grad_rows = grad_pieces.reshape(-1, pieces.shape[-1])
    active_own, slope_own = gelu_parts(
        jnp.dot(row_block, own_up, preferred_element_type=jnp.float32)
    )
    active_other, slope_other = gelu_parts(
        jnp.dot(row_block, other_up, preferred_element_type=jnp.float32)
    )
    total = jnp.dot(
        active_own.astype(jnp.bfloat16), own_down, preferred_element_type=jnp.float32
    ) + jnp.dot(active_other.astype(jnp.bfloat16), other_down, preferred_element_type=jnp.float32)
    back_own = (transposed(grad_rows, own_down) * slope_own).astype(jnp.bfloat16)
    back_other = (transposed(grad_rows, other_down) * slope_other).astype(jnp.bfloat16)
    input_grads = transposed(back_own, own_up) + transposed(back_other, other_up)
    return (
        total.astype(jnp.bfloat16).reshape(pieces.shape),
        input_grads.astype(jnp.bfloat16).reshape(pieces.shape),
    )


def dispatched(
    handoff,
    saved_in,
    grad_handoff,
    route_fwd,
    route_bwd,
    norm_gain,
    router,
    up_proj,
    down_proj,
    moment_m,
    moment_v,
):
    tok_rows = handoff.shape[1]
    feature_dim = handoff.shape[2]
    devices = lax.axis_size("expert")
    experts = devices // 2
    half_cap = max(3, 3 * tok_rows // (2 * experts))
    slot_total = devices * half_cap
    gain_row = norm_gain[0]
    router_table = router[0]
    sender = lax.axis_index("expert")
    entering = shifted(handoff[0], "pipe", 1)
    arriving = shifted(grad_handoff[0], "pipe", -1)
    own_up = up_proj[0]
    own_down = down_proj[0]
    other_up, other_down = from_partner((own_up, own_down), "expert", 0)
    halves = (own_up, other_up, own_down, other_down)
    normed_fwd = normalize(entering, gain_row)[0]
    gates_fwd = route_gates(normed_fwd, router_table, route_fwd[0])[0]
    slots_fwd = slot_plan(route_fwd[0], half_cap, sender)
    send_fwd = pack_rows(jnp.repeat(normed_fwd, 2, axis=0), slots_fwd, slot_total).reshape(
        devices, half_cap, feature_dim
    )
    normed_bwd, scaled_bwd, inv_rms = normalize(saved_in[0], gain_row)
    gates_bwd, picked = route_gates(normed_bwd, router_table, route_bwd[0])
    slots_bwd = slot_plan(route_bwd[0], half_cap, sender)
    send_bwd = pack_rows(jnp.repeat(normed_bwd, 2, axis=0), slots_bwd, slot_total).reshape(
        devices, half_cap, feature_dim
    )
    cotangent = arriving.astype(jnp.float32)
    slot_grads = (
        (gates_bwd[:, :, None] * cotangent[:, None, :])
        .astype(jnp.bfloat16)
        .reshape(-1, feature_dim)
    )
    send_grad = pack_rows(slot_grads, slots_bwd, slot_total).reshape(devices, half_cap, feature_dim)
    back_fwd = lax.all_to_all(
        expert_forward(
            lax.all_to_all(send_fwd, "expert", split_axis=0, concat_axis=0, tiled=True), halves
        ),
        "expert",
        split_axis=0,
        concat_axis=0,
        tiled=True,
    )
    out_second, grad_second = expert_backward(
        lax.all_to_all(send_bwd, "expert", split_axis=0, concat_axis=0, tiled=True),
        lax.all_to_all(send_grad, "expert", split_axis=0, concat_axis=0, tiled=True),
        halves,
    )
    back_bwd = lax.all_to_all(out_second, "expert", split_axis=0, concat_axis=0, tiled=True)
    back_grad = lax.all_to_all(grad_second, "expert", split_axis=0, concat_axis=0, tiled=True)
    out_fwd = (
        back_fwd.reshape(slot_total, feature_dim)[slots_fwd]
        .reshape(tok_rows, 2, feature_dim)
        .astype(jnp.float32)
    )
    segment_sum = (
        entering.astype(jnp.float32)
        + gates_fwd[:, 0:1] * out_fwd[:, 0]
        + gates_fwd[:, 1:2] * out_fwd[:, 1]
    )
    out_bwd = (
        back_bwd.reshape(slot_total, feature_dim)[slots_bwd]
        .reshape(tok_rows, 2, feature_dim)
        .astype(jnp.float32)
    )
    grads_in = (
        back_grad.reshape(slot_total, feature_dim)[slots_bwd]
        .reshape(tok_rows, 2, feature_dim)
        .astype(jnp.float32)
    )
    gate_grads = jnp.sum(cotangent[:, None, :] * out_bwd, axis=2)
    logit_step = gates_bwd[:, 0] * gates_bwd[:, 1] * (gate_grads[:, 0] - gate_grads[:, 1])
    logit_grads = (logit_step[:, None] * (picked[:, 0, :] - picked[:, 1, :])).astype(jnp.bfloat16)
    local_grad = lax.dot_general(
        normed_bwd, logit_grads, (((0,), (0,)), ((), ())), preferred_element_type=jnp.float32
    )
    router_back = transposed(logit_grads, router_table)
    normed_grad = grads_in[:, 0] + grads_in[:, 1] + router_back
    scaled_grad = normed_grad * gain_row
    input_grad = inv_rms * (
        scaled_grad - scaled_bwd * jnp.mean(scaled_grad * scaled_bwd, axis=-1, keepdims=True)
    )
    grad_back = (cotangent + input_grad).astype(jnp.bfloat16)
    row_count = feature_dim // devices
    summed = lax.psum(local_grad, "expert")
    norm_sq = lax.psum(jnp.sum(summed * summed), "pipe")
    grad_rows = lax.dynamic_slice_in_dim(summed, sender * row_count, row_count, 0)
    factor = jnp.minimum(1.0, clip_norm / jnp.sqrt(norm_sq))
    clipped = grad_rows * factor
    new_m = beta_first * moment_m[0] + (1.0 - beta_first) * clipped
    new_v = beta_second * moment_v[0] + (1.0 - beta_second) * clipped * clipped
    first_fix = 1.0 - beta_first**STEP
    second_fix = 1.0 - beta_second**STEP
    router_update = new_m / first_fix / (jnp.sqrt(new_v / second_fix) + 1e-08)
    return (
        segment_sum.astype(jnp.bfloat16)[None],
        grad_back[None],
        new_m[None],
        new_v[None],
        router_update[None],
    )


PIECES = 4
SLOTS = 16
MIB = 2**20


def permuted(value, axes, target):
    sizes = [lax.axis_size(axis) for axis in axes]
    count = math.prod(sizes)
    pairs = []
    for source in range(count):
        place = (source // sizes[-1], source % sizes[-1]) if len(axes) == 2 else (0, source)
        row, column = target(*place)
        pairs.append((source, (row % sizes[0]) * sizes[-1] + column if len(axes) == 2 else column))
    return lax.ppermute(value, axes if len(axes) == 2 else axes[0], pairs)


def normed_rows(block, gain_row):
    widened = block.astype(jnp.float32)
    inv_rms = lax.rsqrt(jnp.mean(widened * widened, axis=-1, keepdims=True) + 1e-05)
    return (widened * inv_rms * gain_row).astype(jnp.bfloat16)


def gates_of(rows, router_rows, routes):
    logits = lax.dot_general(
        rows, router_rows, (((1,), (1,)), ((), ())), preferred_element_type=jnp.float32
    )
    column = lax.broadcasted_iota(jnp.int32, logits.shape, 1)
    first, second = routes[:, 0:1], routes[:, 1:2]
    logit_first = jnp.sum(jnp.where(column == first, logits, 0.0), axis=1, keepdims=True)
    logit_second = jnp.sum(jnp.where(column == second, logits, 0.0), axis=1, keepdims=True)
    gate_first = jax.nn.sigmoid(logit_first - logit_second)
    gate_second = jax.nn.sigmoid(logit_second - logit_first)
    return first, second, gate_first, gate_second


def start_weights(pieces, up_all, down_all, arrived):
    width = up_all.shape[0] // PIECES
    ups, downs = [], []
    for i in range(PIECES):
        part = pl.ds(i * width, width)
        ups.append(
            pltpu.make_async_copy(pieces[i].at[pl.ds(0, width)], up_all.at[part], arrived.at[i])
        )
        downs.append(
            pltpu.make_async_copy(
                pieces[i].at[pl.ds(width, width)], down_all.at[part], arrived.at[PIECES + i]
            )
        )
    for i in range(PIECES):
        ups[i].start()
        downs[i].start()
    return width, ups, downs


def pick(first, second, for_first, for_second, expert):
    return jnp.where(first == expert, for_first, 0.0) + jnp.where(
        second == expert, for_second, 0.0
    )


def forward_kernel(held, next_here, next_there, gain, router_rows, routes, *rest):
    pieces = rest[:PIECES]
    kept, sent, up_all, down_all, entered, rows, hidden, arrived, landed = rest[PIECES:]
    tokens = next_here.shape[0]
    loads = [
        pltpu.make_async_copy(next_here, entered.at[pl.ds(0, tokens)], landed.at[0]),
        pltpu.make_async_copy(next_there, entered.at[pl.ds(tokens, tokens)], landed.at[1]),
    ]
    for load in loads:
        load.start()
    width, ups, downs = start_weights(pieces, up_all, down_all, arrived)
    for load in loads:
        load.wait()
    rows[...] = normed_rows(entered[...], gain[...])
    first, second, gate_first, gate_second = gates_of(rows[...], router_rows[...], routes[...])
    for i in range(PIECES):
        part = slice(i * width, (i + 1) * width)
        ups[i].wait()
        preact = transposed(rows[...], up_all[part, :])
        gate = pick(first, second, gate_first, gate_second, held[2 * i // PIECES])
        hidden[:, part] = (gelu_parts(preact)[0] * gate).astype(jnp.bfloat16)
    for down in downs:
        down.wait()
    block = 512
    for start in range(0, kept.shape[1], block):
        part = slice(start, start + block)
        total = jnp.dot(hidden[...], down_all[:, part], preferred_element_type=jnp.float32)
        kept[:, part] = entered[:tokens, part].astype(jnp.float32) + total[:tokens]
        sent[:, part] = total[tokens:].astype(jnp.bfloat16)


def backward_kernel(
    held, saved_here, saved_there, grad_here, grad_there, gain, router_rows, routes, *rest
):
    pieces = rest[:PIECES]
    (
        kept,
        sent,
        up_all,
        down_all,
        saved,
        grads,
        rows,
        backs,
        arrived,
        landed,
    ) = rest[PIECES:]
    tokens = saved_here.shape[0]
    upper, lower = pl.ds(0, tokens), pl.ds(tokens, tokens)
    loads = [
        pltpu.make_async_copy(saved_here, saved.at[upper], landed.at[0]),
        pltpu.make_async_copy(saved_there, saved.at[lower], landed.at[1]),
        pltpu.make_async_copy(grad_here, grads.at[upper], landed.at[2]),
        pltpu.make_async_copy(grad_there, grads.at[lower], landed.at[3]),
    ]
    for load in loads:
        load.start()
    width, ups, downs = start_weights(pieces, up_all, down_all, arrived)
    for load in loads:
        load.wait()
    rows[...] = normed_rows(saved[...], gain[...])
    first, second, gate_first, gate_second = gates_of(rows[...], router_rows[...], routes[...])
    signed_sum = jnp.zeros_like(gate_first)
    for i in range(PIECES):
        expert = held[2 * i // PIECES]
        part = slice(i * width, (i + 1) * width)
        ups[i].wait()
        preact = transposed(rows[...], up_all[part, :])
        downs[i].wait()
        hidden_grad = transposed(grads[...], down_all[part, :])
        active, slope = gelu_parts(preact)
        active = active.astype(jnp.bfloat16).astype(jnp.float32)
        signed_sum += pick(first, second, 1.0, -1.0, expert) * jnp.sum(
            active * hidden_grad, axis=1, keepdims=True
        )
        gate = pick(first, second, gate_first, gate_second, expert)
        backs[:, part] = (hidden_grad * slope * gate).astype(jnp.bfloat16)
    step = gate_first * gate_second * signed_sum
    column = lax.broadcasted_iota(jnp.int32, (2 * tokens, SLOTS), 1)
    expert = jnp.where(column < SLOTS // 4, column, column - SLOTS // 4)
    step = pick(first, second, step, -step, expert)
    coarse = step.astype(jnp.bfloat16).astype(jnp.float32)
    logit_grads = jnp.where(column < SLOTS // 4, coarse, step - coarse)
    logit_grads = jnp.where(column < SLOTS // 2, logit_grads, 0.0).astype(jnp.bfloat16)
    block = 512
    for start in range(0, kept.shape[1], block):
        part = slice(start, start + block)
        parts = lax.dot_general(
            logit_grads,
            rows[:, part],
            (((0,), (0,)), ((), ())),
            preferred_element_type=jnp.float32,
        )
        parts = parts + pltpu.roll(parts, SLOTS - SLOTS // 4, 0)
        high = parts.astype(jnp.bfloat16).astype(jnp.float32)
        low = pltpu.roll(parts - high, SLOTS // 4, 0)
        row = lax.broadcasted_iota(jnp.int32, parts.shape, 0)
        sent[tokens : tokens + SLOTS, part] = jnp.where(
            row < SLOTS // 4, high, low
        ).astype(jnp.bfloat16)
        total = jnp.dot(
            backs[...], up_all[:, part], preferred_element_type=jnp.float32
        ) + jnp.dot(logit_grads, router_rows[:, part], preferred_element_type=jnp.float32)
        kept[:, part] = total[:tokens]
        sent[:tokens, part] = total[tokens:].astype(jnp.bfloat16)


def closing_kernel(saved, arriving, gain, kept, came, out):
    widened = saved[...].astype(jnp.float32)
    inv_rms = lax.rsqrt(jnp.mean(widened * widened, axis=-1, keepdims=True) + 1e-05)
    scaled = widened * inv_rms
    scaled_grad = (kept[...] + came[...].astype(jnp.float32)) * gain[...]
    mean = jnp.mean(scaled_grad * scaled, axis=-1, keepdims=True)
    input_grad = inv_rms * (scaled_grad - scaled * mean)
    out[...] = (arriving[...].astype(jnp.float32) + input_grad).astype(jnp.bfloat16)


def in_hbm(count):
    return [pl.BlockSpec(memory_space=pltpu.HBM)] * count


def in_vmem(count):
    return [pl.BlockSpec(memory_space=pltpu.VMEM)] * count


def run_experts(kernel, held, blocks, gain, router_rows, routes, pieces, matmuls, more_rows):
    tokens, features = blocks[0].shape
    hidden = PIECES * pieces[0].shape[0] // 2
    weights = pltpu.VMEM((hidden, features), jnp.bfloat16)
    rows = pltpu.VMEM((2 * tokens, features), jnp.bfloat16)
    return pl.pallas_call(
        kernel,
        out_shape=(
            jax.ShapeDtypeStruct((tokens, features), jnp.float32),
            jax.ShapeDtypeStruct((tokens + more_rows, features), jnp.bfloat16),
        ),
        in_specs=[pl.BlockSpec(memory_space=pltpu.SMEM)]
        + in_hbm(len(blocks))
        + in_vmem(3)
        + in_hbm(PIECES),
        out_specs=tuple(in_vmem(2)),
        scratch_shapes=[
            weights,
            weights,
            *[rows] * (len(blocks) // 2 + 1),
            pltpu.VMEM((2 * tokens, hidden), jnp.bfloat16),
            pltpu.SemaphoreType.DMA((2 * PIECES,)),
            pltpu.SemaphoreType.DMA((len(blocks),)),
        ],
        compiler_params=pltpu.CompilerParams(vmem_limit_bytes=60 * MIB),
        cost_estimate=pl.CostEstimate(
            flops=4 * matmuls * tokens * features * hidden,
            bytes_accessed=4 * features * hidden + 16 * tokens * features,
            transcendentals=2 * tokens * hidden,
        ),
    )(held, *blocks, gain, router_rows, routes, *pieces)


def run_closing(saved, arriving, gain, kept, came):
    tokens, features = saved.shape
    block = tokens // 4
    rows = pl.BlockSpec((block, features), lambda i: (i, 0))
    return pl.pallas_call(
        closing_kernel,
        out_shape=jax.ShapeDtypeStruct((tokens, features), jnp.bfloat16),
        grid=(4,),
        in_specs=[
            rows,
            rows,
            pl.BlockSpec((1, features), lambda i: (0, 0)),
            rows,
            rows,
        ],
        out_specs=rows,
        cost_estimate=pl.CostEstimate(
            flops=16 * tokens * features, bytes_accessed=12 * tokens * features, transcendentals=0
        ),
    )(saved, arriving, gain, kept, came)


def after(value, *earlier):
    return lax.optimization_barrier((value, *earlier))[0]


def paired(
    handoff,
    saved_in,
    grad_handoff,
    route_fwd,
    route_bwd,
    norm_gain,
    router,
    up_proj,
    down_proj,
    moment_m,
    moment_v,
):
    def shift(value, by):
        return permuted(value, both, lambda row, place: (row + by, place))

    def mirror(value, by=0):
        if by == 0:
            return permuted(value, line, lambda row, place: (row, place ^ 6))
        return permuted(value, both, lambda row, place: (row + by, place ^ 6))

    def near(value):
        return permuted(value, line, lambda row, place: (row, place ^ 2))

    def across(value):
        return permuted(value, line, lambda row, place: (row, place ^ 1))

    both, line = ("pipe", "expert"), ("expert",)
    sender = lax.axis_index("expert")
    saved, leaving, cotangent = saved_in[0], handoff[0], grad_handoff[0]
    routes = jnp.concatenate([route_fwd[0].T, route_bwd[0].T], axis=0)
    routes_there = mirror(routes)
    own = jnp.concatenate([up_proj[0].T, down_proj[0]], axis=0)
    close = near(own)
    own_other = across(own)
    saved_there = mirror(saved)
    entering = shift(leaving, 1)
    arriving = shift(cotangent, -1)
    arriving_there = mirror(after(arriving, own_other, entering, saved_there))
    entering_there = mirror(after(entering, own_other, arriving, saved_there))
    close_other = across(after(close, arriving_there, routes_there))
    pieces = (own, own_other, close, close_other)
    all_routes = jnp.concatenate([routes, routes_there], axis=1)
    chip = sender // 2
    held = jnp.stack([chip, chip ^ 1]).astype(jnp.int32)
    router_turned = router[0].T
    router_rows = jnp.concatenate(
        [router_turned, router_turned, jnp.zeros((SLOTS // 2, router_turned.shape[1]), jnp.bfloat16)]
    )
    quarter = SLOTS // 4
    kept_bwd, sent_bwd = run_experts(
        backward_kernel,
        held,
        (saved, saved_there, arriving, arriving_there),
        norm_gain,
        router_rows,
        all_routes[2:].T,
        pieces,
        3,
        SLOTS,
    )
    came_bwd = mirror(sent_bwd)
    kept_fwd, sent_fwd = run_experts(
        forward_kernel,
        held,
        (entering, after(entering_there, sent_bwd)),
        norm_gain,
        router_rows,
        all_routes[:2].T,
        pieces,
        2,
        0,
    )
    came_fwd = mirror(sent_fwd)
    grad_back = run_closing(saved, arriving, norm_gain, kept_bwd, came_bwd)
    tokens = saved.shape[0]
    terms = sent_bwd[tokens:].astype(jnp.float32) + came_bwd[tokens:].astype(jnp.float32)
    terms = terms[:quarter] + terms[quarter : 2 * quarter]
    devices = lax.axis_size("expert")
    four = devices // 2
    terms = jnp.broadcast_to(terms[None], (four, *terms.shape))
    groups = [[first * four + i for i in range(four)] for first in range(2)]
    terms = lax.all_to_all(
        terms, "expert", split_axis=0, concat_axis=0, tiled=True, axis_index_groups=groups
    )
    summed = jnp.sum(terms, axis=0)
    square = jnp.broadcast_to(jnp.sum(summed * summed), (lax.axis_size("pipe"), 128))
    square = lax.all_to_all(square, "pipe", split_axis=0, concat_axis=0, tiled=True)
    norm_sq = jnp.sum(square[:, 0])
    width = summed.shape[1] // devices
    grad_rows = lax.dynamic_slice_in_dim(summed, sender * width, width, 1).T
    factor = jnp.minimum(1.0, clip_norm / jnp.sqrt(norm_sq))
    clipped = grad_rows * factor
    new_m = beta_first * moment_m[0] + (1.0 - beta_first) * clipped
    new_v = beta_second * moment_v[0] + (1.0 - beta_second) * clipped * clipped
    first_fix = 1.0 - beta_first**STEP
    second_fix = 1.0 - beta_second**STEP
    router_update = new_m / first_fix / (jnp.sqrt(new_v / second_fix) + 1e-08)
    segment_out = (kept_fwd + came_fwd.astype(jnp.float32)).astype(jnp.bfloat16)
    return (
        segment_out[None],
        grad_back[None],
        new_m[None],
        new_v[None],
        router_update[None],
    )


def solution(mesh):
    in_specs = (
        P("pipe", "expert", None),
        P("pipe", "expert", None),
        P("pipe", "expert", None),
        P("pipe", "expert", None),
        P("pipe", "expert", None),
        P("pipe", None),
        P("pipe", None, None),
        P("pipe", None, "expert"),
        P("pipe", "expert", None),
        P("pipe", "expert", None),
        P("pipe", "expert", None),
    )
    out_specs = (
        P("pipe", "expert", None),
        P("pipe", "expert", None),
        P("pipe", "expert", None),
        P("pipe", "expert", None),
        P("pipe", "expert", None),
    )
    experts_held = mesh.shape["expert"] // 2
    return jax.shard_map(
        paired if experts_held == 4 else dispatched, mesh=mesh, in_specs=in_specs, out_specs=out_specs, check_vma=False
    )
```

```python
import math

import jax
import jax.numpy as jnp
from jax import lax
from jax.experimental import pallas as pl
from jax.experimental.pallas import tpu as pltpu
from jax.sharding import PartitionSpec as P

STEP = 10


gelu_scale = math.sqrt(2.0 / math.pi)
beta_first = 0.9
beta_second = 0.95
clip_norm = 1.0


def shifted(x, axis, by):
    length = lax.axis_size(axis)
    return lax.ppermute(x, axis, [(i, (i + by) % length) for i in range(length)])


def from_partner(value, axis, bit):
    mask = 2**bit
    pairs = [(source, source ^ mask) for source in range(lax.axis_size(axis))]
    return lax.ppermute(value, axis, pairs)


def gelu_parts(preact):
    square = preact * preact
    tangent = jnp.tanh(gelu_scale * (preact + 0.044715 * square * preact))
    activated = 0.5 * preact * (1.0 + tangent)
    gelu_slope = 0.5 * (1.0 + tangent) + 0.5 * preact * (1.0 - tangent * tangent) * gelu_scale * (
        1.0 + 0.134145 * square
    )
    return (activated, gelu_slope)


def normalize(inputs, gain_row):
    widened = inputs.astype(jnp.float32)
    inv_rms = lax.rsqrt(jnp.mean(widened * widened, axis=-1, keepdims=True) + 1e-05)
    scaled = widened * inv_rms
    return ((scaled * gain_row).astype(jnp.bfloat16), scaled, inv_rms)


def route_gates(normed, router_table, routes):
    logits = jnp.dot(normed, router_table, preferred_element_type=jnp.float32)
    columns = jnp.arange(router_table.shape[1], dtype=jnp.int32)
    picked = (routes[:, :, None] == columns[None, None, :]).astype(jnp.float32)
    chosen = jnp.sum(logits[:, None, :] * picked, axis=2)
    first_gate = jax.nn.sigmoid(chosen[:, 0] - chosen[:, 1])
    second = jax.nn.sigmoid(chosen[:, 1] - chosen[:, 0])
    return (jnp.stack([first_gate, second], axis=1), picked)


def slot_plan(routes, half_cap, sender):
    flat_routes = routes.reshape(-1)
    rows = jnp.arange(flat_routes.shape[0], dtype=jnp.int32)
    before = (rows[:, None] > rows[None, :]) & (flat_routes[:, None] == flat_routes[None, :])
    position = jnp.sum(before.astype(jnp.int32), axis=1)
    target = 2 * flat_routes + (position + sender) % 2
    return target * half_cap + position // 2


def pack_rows(row_block, slots, slot_total):
    blank_rows = jnp.zeros((slot_total, row_block.shape[1]), row_block.dtype)
    return blank_rows.at[slots].set(row_block)


def transposed(left, right):
    return lax.dot_general(
        left, right, (((1,), (1,)), ((), ())), preferred_element_type=jnp.float32
    )


def expert_forward(pieces, halves):
    own_up, other_up, own_down, other_down = halves
    row_block = pieces.reshape(-1, pieces.shape[-1])
    active_own = gelu_parts(jnp.dot(row_block, own_up, preferred_element_type=jnp.float32))[
        0
    ].astype(jnp.bfloat16)
    active_other = gelu_parts(jnp.dot(row_block, other_up, preferred_element_type=jnp.float32))[
        0
    ].astype(jnp.bfloat16)
    total = jnp.dot(active_own, own_down, preferred_element_type=jnp.float32) + jnp.dot(
        active_other, other_down, preferred_element_type=jnp.float32
    )
    return total.astype(jnp.bfloat16).reshape(pieces.shape)


def expert_backward(pieces, grad_pieces, halves):
    own_up, other_up, own_down, other_down = halves
    row_block = pieces.reshape(-1, pieces.shape[-1])
    grad_rows = grad_pieces.reshape(-1, pieces.shape[-1])
    active_own, slope_own = gelu_parts(
        jnp.dot(row_block, own_up, preferred_element_type=jnp.float32)
    )
    active_other, slope_other = gelu_parts(
        jnp.dot(row_block, other_up, preferred_element_type=jnp.float32)
    )
    total = jnp.dot(
        active_own.astype(jnp.bfloat16), own_down, preferred_element_type=jnp.float32
    ) + jnp.dot(active_other.astype(jnp.bfloat16), other_down, preferred_element_type=jnp.float32)
    back_own = (transposed(grad_rows, own_down) * slope_own).astype(jnp.bfloat16)
    back_other = (transposed(grad_rows, other_down) * slope_other).astype(jnp.bfloat16)
    input_grads = transposed(back_own, own_up) + transposed(back_other, other_up)
    return (
        total.astype(jnp.bfloat16).reshape(pieces.shape),
        input_grads.astype(jnp.bfloat16).reshape(pieces.shape),
    )


def dispatched(
    handoff,
    saved_in,
    grad_handoff,
    route_fwd,
    route_bwd,
    norm_gain,
    router,
    up_proj,
    down_proj,
    moment_m,
    moment_v,
):
    tok_rows = handoff.shape[1]
    feature_dim = handoff.shape[2]
    devices = lax.axis_size("expert")
    experts = devices // 2
    half_cap = max(3, 3 * tok_rows // (2 * experts))
    slot_total = devices * half_cap
    gain_row = norm_gain[0]
    router_table = router[0]
    sender = lax.axis_index("expert")
    entering = shifted(handoff[0], "pipe", 1)
    arriving = shifted(grad_handoff[0], "pipe", -1)
    own_up = up_proj[0]
    own_down = down_proj[0]
    other_up, other_down = from_partner((own_up, own_down), "expert", 0)
    halves = (own_up, other_up, own_down, other_down)
    normed_fwd = normalize(entering, gain_row)[0]
    gates_fwd = route_gates(normed_fwd, router_table, route_fwd[0])[0]
    slots_fwd = slot_plan(route_fwd[0], half_cap, sender)
    send_fwd = pack_rows(jnp.repeat(normed_fwd, 2, axis=0), slots_fwd, slot_total).reshape(
        devices, half_cap, feature_dim
    )
    normed_bwd, scaled_bwd, inv_rms = normalize(saved_in[0], gain_row)
    gates_bwd, picked = route_gates(normed_bwd, router_table, route_bwd[0])
    slots_bwd = slot_plan(route_bwd[0], half_cap, sender)
    send_bwd = pack_rows(jnp.repeat(normed_bwd, 2, axis=0), slots_bwd, slot_total).reshape(
        devices, half_cap, feature_dim
    )
    cotangent = arriving.astype(jnp.float32)
    slot_grads = (
        (gates_bwd[:, :, None] * cotangent[:, None, :])
        .astype(jnp.bfloat16)
        .reshape(-1, feature_dim)
    )
    send_grad = pack_rows(slot_grads, slots_bwd, slot_total).reshape(devices, half_cap, feature_dim)
    back_fwd = lax.all_to_all(
        expert_forward(
            lax.all_to_all(send_fwd, "expert", split_axis=0, concat_axis=0, tiled=True), halves
        ),
        "expert",
        split_axis=0,
        concat_axis=0,
        tiled=True,
    )
    out_second, grad_second = expert_backward(
        lax.all_to_all(send_bwd, "expert", split_axis=0, concat_axis=0, tiled=True),
        lax.all_to_all(send_grad, "expert", split_axis=0, concat_axis=0, tiled=True),
        halves,
    )
    back_bwd = lax.all_to_all(out_second, "expert", split_axis=0, concat_axis=0, tiled=True)
    back_grad = lax.all_to_all(grad_second, "expert", split_axis=0, concat_axis=0, tiled=True)
    out_fwd = (
        back_fwd.reshape(slot_total, feature_dim)[slots_fwd]
        .reshape(tok_rows, 2, feature_dim)
        .astype(jnp.float32)
    )
    segment_sum = (
        entering.astype(jnp.float32)
        + gates_fwd[:, 0:1] * out_fwd[:, 0]
        + gates_fwd[:, 1:2] * out_fwd[:, 1]
    )
    out_bwd = (
        back_bwd.reshape(slot_total, feature_dim)[slots_bwd]
        .reshape(tok_rows, 2, feature_dim)
        .astype(jnp.float32)
    )
    grads_in = (
        back_grad.reshape(slot_total, feature_dim)[slots_bwd]
        .reshape(tok_rows, 2, feature_dim)
        .astype(jnp.float32)
    )
    gate_grads = jnp.sum(cotangent[:, None, :] * out_bwd, axis=2)
    logit_step = gates_bwd[:, 0] * gates_bwd[:, 1] * (gate_grads[:, 0] - gate_grads[:, 1])
    logit_grads = (logit_step[:, None] * (picked[:, 0, :] - picked[:, 1, :])).astype(jnp.bfloat16)
    local_grad = lax.dot_general(
        normed_bwd, logit_grads, (((0,), (0,)), ((), ())), preferred_element_type=jnp.float32
    )
    router_back = transposed(logit_grads, router_table)
    normed_grad = grads_in[:, 0] + grads_in[:, 1] + router_back
    scaled_grad = normed_grad * gain_row
    input_grad = inv_rms * (
        scaled_grad - scaled_bwd * jnp.mean(scaled_grad * scaled_bwd, axis=-1, keepdims=True)
    )
    grad_back = (cotangent + input_grad).astype(jnp.bfloat16)
    row_count = feature_dim // devices
    summed = lax.psum(local_grad, "expert")
    norm_sq = lax.psum(jnp.sum(summed * summed), "pipe")
    grad_rows = lax.dynamic_slice_in_dim(summed, sender * row_count, row_count, 0)
    factor = jnp.minimum(1.0, clip_norm / jnp.sqrt(norm_sq))
    clipped = grad_rows * factor
    new_m = beta_first * moment_m[0] + (1.0 - beta_first) * clipped
    new_v = beta_second * moment_v[0] + (1.0 - beta_second) * clipped * clipped
    first_fix = 1.0 - beta_first**STEP
    second_fix = 1.0 - beta_second**STEP
    router_update = new_m / first_fix / (jnp.sqrt(new_v / second_fix) + 1e-08)
    return (
        segment_sum.astype(jnp.bfloat16)[None],
        grad_back[None],
        new_m[None],
        new_v[None],
        router_update[None],
    )


PIECES = 4
SLOTS = 16
MIB = 2**20


def permuted(value, axes, target):
    sizes = [lax.axis_size(axis) for axis in axes]
    count = math.prod(sizes)
    pairs = []
    for source in range(count):
        place = (source // sizes[-1], source % sizes[-1]) if len(axes) == 2 else (0, source)
        row, column = target(*place)
        pairs.append((source, (row % sizes[0]) * sizes[-1] + column if len(axes) == 2 else column))
    return lax.ppermute(value, axes if len(axes) == 2 else axes[0], pairs)


def normed_rows(block, gain_row):
    widened = block.astype(jnp.float32)
    inv_rms = lax.rsqrt(jnp.mean(widened * widened, axis=-1, keepdims=True) + 1e-05)
    return (widened * inv_rms * gain_row).astype(jnp.bfloat16)


def gates_of(rows, router_rows, routes):
    logits = lax.dot_general(
        rows, router_rows, (((1,), (1,)), ((), ())), preferred_element_type=jnp.float32
    )
    column = lax.broadcasted_iota(jnp.int32, logits.shape, 1)
    first, second = routes[:, 0:1], routes[:, 1:2]
    logit_first = jnp.sum(jnp.where(column == first, logits, 0.0), axis=1, keepdims=True)
    logit_second = jnp.sum(jnp.where(column == second, logits, 0.0), axis=1, keepdims=True)
    gate_first = jax.nn.sigmoid(logit_first - logit_second)
    gate_second = jax.nn.sigmoid(logit_second - logit_first)
    return first, second, gate_first, gate_second


def start_weights(pieces, up_all, down_all, arrived):
    width = up_all.shape[0] // PIECES
    ups, downs = [], []
    for i in range(PIECES):
        part = pl.ds(i * width, width)
        ups.append(
            pltpu.make_async_copy(pieces[i].at[pl.ds(0, width)], up_all.at[part], arrived.at[i])
        )
        downs.append(
            pltpu.make_async_copy(
                pieces[i].at[pl.ds(width, width)], down_all.at[part], arrived.at[PIECES + i]
            )
        )
    for i in range(PIECES):
        ups[i].start()
        downs[i].start()
    return width, ups, downs


def pick(first, second, for_first, for_second, expert):
    return jnp.where(first == expert, for_first, 0.0) + jnp.where(
        second == expert, for_second, 0.0
    )


def forward_kernel(held, next_here, next_there, gain, router_rows, routes, *rest):
    pieces = rest[:PIECES]
    kept, sent, up_all, down_all, entered, rows, hidden, arrived, landed = rest[PIECES:]
    tokens = next_here.shape[0]
    loads = [
        pltpu.make_async_copy(next_here, entered.at[pl.ds(0, tokens)], landed.at[0]),
        pltpu.make_async_copy(next_there.at[pl.ds(0, tokens)], entered.at[pl.ds(tokens, tokens)], landed.at[1]),
    ]
    for load in loads:
        load.start()
    width, ups, downs = start_weights(pieces, up_all, down_all, arrived)
    for load in loads:
        load.wait()
    rows[...] = normed_rows(entered[...], gain[...])
    first, second, gate_first, gate_second = gates_of(rows[...], router_rows[...], routes[...])
    for i in range(PIECES):
        part = slice(i * width, (i + 1) * width)
        ups[i].wait()
        preact = transposed(rows[...], up_all[part, :])
        gate = pick(first, second, gate_first, gate_second, held[2 * i // PIECES])
        hidden[:, part] = (gelu_parts(preact)[0] * gate).astype(jnp.bfloat16)
    for down in downs:
        down.wait()
    block = 512
    for start in range(0, kept.shape[1], block):
        part = slice(start, start + block)
        total = jnp.dot(hidden[...], down_all[:, part], preferred_element_type=jnp.float32)
        kept[:, part] = entered[:tokens, part].astype(jnp.float32) + total[:tokens]
        sent[:, part] = total[tokens:].astype(jnp.bfloat16)


def backward_kernel(
    held, saved_here, saved_there, grad_here, grad_there, gain, router_rows, routes, *rest
):
    pieces = rest[:PIECES]
    (
        kept,
        sent,
        up_all,
        down_all,
        saved,
        grads,
        rows,
        backs,
        arrived,
        landed,
    ) = rest[PIECES:]
    tokens = saved_here.shape[0]
    upper, lower = pl.ds(0, tokens), pl.ds(tokens, tokens)
    loads = [
        pltpu.make_async_copy(saved_here, saved.at[upper], landed.at[0]),
        pltpu.make_async_copy(saved_there, saved.at[lower], landed.at[1]),
        pltpu.make_async_copy(grad_here, grads.at[upper], landed.at[2]),
        pltpu.make_async_copy(grad_there, grads.at[lower], landed.at[3]),
    ]
    for load in loads:
        load.start()
    width, ups, downs = start_weights(pieces, up_all, down_all, arrived)
    for load in loads:
        load.wait()
    rows[...] = normed_rows(saved[...], gain[...])
    first, second, gate_first, gate_second = gates_of(rows[...], router_rows[...], routes[...])
    signed_sum = jnp.zeros_like(gate_first)
    for i in range(PIECES):
        expert = held[2 * i // PIECES]
        part = slice(i * width, (i + 1) * width)
        ups[i].wait()
        preact = transposed(rows[...], up_all[part, :])
        downs[i].wait()
        hidden_grad = transposed(grads[...], down_all[part, :])
        active, slope = gelu_parts(preact)
        active = active.astype(jnp.bfloat16).astype(jnp.float32)
        signed_sum += pick(first, second, 1.0, -1.0, expert) * jnp.sum(
            active * hidden_grad, axis=1, keepdims=True
        )
        gate = pick(first, second, gate_first, gate_second, expert)
        backs[:, part] = (hidden_grad * slope * gate).astype(jnp.bfloat16)
    step = gate_first * gate_second * signed_sum
    column = lax.broadcasted_iota(jnp.int32, (2 * tokens, SLOTS), 1)
    expert = jnp.where(column < SLOTS // 4, column, column - SLOTS // 4)
    step = pick(first, second, step, -step, expert)
    coarse = step.astype(jnp.bfloat16).astype(jnp.float32)
    logit_grads = jnp.where(column < SLOTS // 4, coarse, step - coarse)
    logit_grads = jnp.where(column < SLOTS // 2, logit_grads, 0.0).astype(jnp.bfloat16)
    block = 512
    for start in range(0, kept.shape[1], block):
        part = slice(start, start + block)
        parts = lax.dot_general(
            logit_grads,
            rows[:, part],
            (((0,), (0,)), ((), ())),
            preferred_element_type=jnp.float32,
        )
        parts = parts + pltpu.roll(parts, SLOTS - SLOTS // 4, 0)
        high = parts.astype(jnp.bfloat16).astype(jnp.float32)
        low = pltpu.roll(parts - high, SLOTS // 4, 0)
        row = lax.broadcasted_iota(jnp.int32, parts.shape, 0)
        sent[tokens : tokens + SLOTS, part] = jnp.where(
            row < SLOTS // 4, high, low
        ).astype(jnp.bfloat16)
        total = jnp.dot(
            backs[...], up_all[:, part], preferred_element_type=jnp.float32
        ) + jnp.dot(logit_grads, router_rows[:, part], preferred_element_type=jnp.float32)
        kept[:, part] = total[:tokens]
        sent[:tokens, part] = total[tokens:].astype(jnp.bfloat16)


def closing_kernel(saved, arriving, gain, kept, came, out):
    widened = saved[...].astype(jnp.float32)
    inv_rms = lax.rsqrt(jnp.mean(widened * widened, axis=-1, keepdims=True) + 1e-05)
    scaled = widened * inv_rms
    scaled_grad = (kept[...] + came[...].astype(jnp.float32)) * gain[...]
    mean = jnp.mean(scaled_grad * scaled, axis=-1, keepdims=True)
    input_grad = inv_rms * (scaled_grad - scaled * mean)
    out[...] = (arriving[...].astype(jnp.float32) + input_grad).astype(jnp.bfloat16)


def in_hbm(count):
    return [pl.BlockSpec(memory_space=pltpu.HBM)] * count


def in_vmem(count):
    return [pl.BlockSpec(memory_space=pltpu.VMEM)] * count


def run_experts(kernel, held, blocks, gain, router_rows, routes, pieces, matmuls, more_rows):
    tokens, features = blocks[0].shape
    hidden = PIECES * pieces[0].shape[0] // 2
    weights = pltpu.VMEM((hidden, features), jnp.bfloat16)
    rows = pltpu.VMEM((2 * tokens, features), jnp.bfloat16)
    return pl.pallas_call(
        kernel,
        out_shape=(
            jax.ShapeDtypeStruct((tokens, features), jnp.float32),
            jax.ShapeDtypeStruct((tokens + more_rows, features), jnp.bfloat16),
        ),
        in_specs=[pl.BlockSpec(memory_space=pltpu.SMEM)]
        + in_hbm(len(blocks))
        + in_vmem(3)
        + in_hbm(PIECES),
        out_specs=tuple(in_vmem(2)),
        scratch_shapes=[
            weights,
            weights,
            *[rows] * (len(blocks) // 2 + 1),
            pltpu.VMEM((2 * tokens, hidden), jnp.bfloat16),
            pltpu.SemaphoreType.DMA((2 * PIECES,)),
            pltpu.SemaphoreType.DMA((len(blocks),)),
        ],
        compiler_params=pltpu.CompilerParams(vmem_limit_bytes=60 * MIB),
        cost_estimate=pl.CostEstimate(
            flops=4 * matmuls * tokens * features * hidden,
            bytes_accessed=4 * features * hidden + 16 * tokens * features,
            transcendentals=2 * tokens * hidden,
        ),
    )(held, *blocks, gain, router_rows, routes, *pieces)


def run_closing(saved, arriving, gain, kept, came):
    tokens, features = saved.shape
    block = tokens // 4
    rows = pl.BlockSpec((block, features), lambda i: (i, 0))
    return pl.pallas_call(
        closing_kernel,
        out_shape=jax.ShapeDtypeStruct((tokens, features), jnp.bfloat16),
        grid=(4,),
        in_specs=[
            rows,
            rows,
            pl.BlockSpec((1, features), lambda i: (0, 0)),
            rows,
            rows,
        ],
        out_specs=rows,
        cost_estimate=pl.CostEstimate(
            flops=16 * tokens * features, bytes_accessed=12 * tokens * features, transcendentals=0
        ),
    )(saved, arriving, gain, kept, came)


def after(value, *earlier):
    return lax.optimization_barrier((value, *earlier))[0]


def paired(
    handoff,
    saved_in,
    grad_handoff,
    route_fwd,
    route_bwd,
    norm_gain,
    router,
    up_proj,
    down_proj,
    moment_m,
    moment_v,
):
    def shift(value, by):
        return permuted(value, both, lambda row, place: (row + by, place))

    def mirror(value, by=0):
        if by == 0:
            return permuted(value, line, lambda row, place: (row, place ^ 6))
        return permuted(value, both, lambda row, place: (row + by, place ^ 6))

    def near(value):
        return permuted(value, line, lambda row, place: (row, place ^ 2))

    def across(value):
        return permuted(value, line, lambda row, place: (row, place ^ 1))

    both, line = ("pipe", "expert"), ("expert",)
    sender = lax.axis_index("expert")
    saved, leaving, cotangent = saved_in[0], handoff[0], grad_handoff[0]
    routes = jnp.concatenate([route_fwd[0].T, route_bwd[0].T], axis=0)
    tokens, features = saved.shape
    listed = jnp.pad(
        routes.astype(jnp.bfloat16), ((0, SLOTS - routes.shape[0]), (0, features - tokens))
    )
    saved_there = mirror(saved)
    entering = shift(leaving, 1)
    arriving = shift(after(cotangent, entering), -1)
    own = jnp.concatenate([up_proj[0].T, down_proj[0]], axis=0)
    close = near(own)
    own_other = across(own)
    arriving_there = mirror(after(arriving, own_other, saved_there))
    entering_there = mirror(jnp.concatenate([entering, listed], axis=0), 0)
    routes_there = entering_there[tokens : tokens + routes.shape[0], :tokens].astype(jnp.int32)
    close_other = across(after(close, arriving_there, entering_there))
    pieces = (own, own_other, close, close_other)
    all_routes = jnp.concatenate([routes, routes_there], axis=1)
    chip = sender // 2
    held = jnp.stack([chip, chip ^ 1]).astype(jnp.int32)
    router_turned = router[0].T
    router_rows = jnp.concatenate(
        [router_turned, router_turned, jnp.zeros((SLOTS // 2, router_turned.shape[1]), jnp.bfloat16)]
    )
    quarter = SLOTS // 4
    kept_bwd, sent_bwd = run_experts(
        backward_kernel,
        held,
        (saved, saved_there, arriving, arriving_there),
        norm_gain,
        router_rows,
        all_routes[2:].T,
        pieces,
        3,
        SLOTS,
    )
    came_bwd = mirror(sent_bwd)
    kept_fwd, sent_fwd = run_experts(
        forward_kernel,
        held,
        (entering, after(entering_there, sent_bwd)),
        norm_gain,
        router_rows,
        all_routes[:2].T,
        pieces,
        2,
        0,
    )
    came_fwd = mirror(sent_fwd)
    grad_back = run_closing(saved, arriving, norm_gain, kept_bwd, came_bwd)
    terms = sent_bwd[tokens:].astype(jnp.float32) + came_bwd[tokens:].astype(jnp.float32)
    terms = terms[:quarter] + terms[quarter : 2 * quarter]
    devices = lax.axis_size("expert")
    four = devices // 2
    terms = after(jnp.broadcast_to(terms[None], (four, *terms.shape)), grad_back)
    groups = [[first * four + i for i in range(four)] for first in range(2)]
    terms = lax.all_to_all(
        terms, "expert", split_axis=0, concat_axis=0, tiled=True, axis_index_groups=groups
    )
    summed = jnp.sum(terms, axis=0)
    square = jnp.broadcast_to(jnp.sum(summed * summed), (lax.axis_size("pipe"), 128))
    square = lax.all_to_all(square, "pipe", split_axis=0, concat_axis=0, tiled=True)
    norm_sq = jnp.sum(square[:, 0])
    width = summed.shape[1] // devices
    grad_rows = lax.dynamic_slice_in_dim(summed, sender * width, width, 1).T
    factor = jnp.minimum(1.0, clip_norm / jnp.sqrt(norm_sq))
    clipped = grad_rows * factor
    new_m = beta_first * moment_m[0] + (1.0 - beta_first) * clipped
    new_v = beta_second * moment_v[0] + (1.0 - beta_second) * clipped * clipped
    first_fix = 1.0 - beta_first**STEP
    second_fix = 1.0 - beta_second**STEP
    router_update = new_m / first_fix / (jnp.sqrt(new_v / second_fix) + 1e-08)
    segment_out = (kept_fwd + came_fwd.astype(jnp.float32)).astype(jnp.bfloat16)
    return (
        segment_out[None],
        grad_back[None],
        new_m[None],
        new_v[None],
        router_update[None],
    )


def solution(mesh):
    in_specs = (
        P("pipe", "expert", None),
        P("pipe", "expert", None),
        P("pipe", "expert", None),
        P("pipe", "expert", None),
        P("pipe", "expert", None),
        P("pipe", None),
        P("pipe", None, None),
        P("pipe", None, "expert"),
        P("pipe", "expert", None),
        P("pipe", "expert", None),
        P("pipe", "expert", None),
    )
    out_specs = (
        P("pipe", "expert", None),
        P("pipe", "expert", None),
        P("pipe", "expert", None),
        P("pipe", "expert", None),
        P("pipe", "expert", None),
    )
    experts_held = mesh.shape["expert"] // 2
    return jax.shard_map(
        paired if experts_held == 4 else dispatched, mesh=mesh, in_specs=in_specs, out_specs=out_specs, check_vma=False
    )
```

```python
import math

import jax
import jax.numpy as jnp
from jax import lax
from jax.experimental import pallas as pl
from jax.experimental.pallas import tpu as pltpu
from jax.sharding import PartitionSpec as P

STEP = 10


gelu_scale = math.sqrt(2.0 / math.pi)
beta_first = 0.9
beta_second = 0.95
clip_norm = 1.0


def shifted(x, axis, by):
    length = lax.axis_size(axis)
    return lax.ppermute(x, axis, [(i, (i + by) % length) for i in range(length)])


def from_partner(value, axis, bit):
    mask = 2**bit
    pairs = [(source, source ^ mask) for source in range(lax.axis_size(axis))]
    return lax.ppermute(value, axis, pairs)


def gelu_parts(preact):
    square = preact * preact
    tangent = jnp.tanh(gelu_scale * (preact + 0.044715 * square * preact))
    activated = 0.5 * preact * (1.0 + tangent)
    gelu_slope = 0.5 * (1.0 + tangent) + 0.5 * preact * (1.0 - tangent * tangent) * gelu_scale * (
        1.0 + 0.134145 * square
    )
    return (activated, gelu_slope)


def normalize(inputs, gain_row):
    widened = inputs.astype(jnp.float32)
    inv_rms = lax.rsqrt(jnp.mean(widened * widened, axis=-1, keepdims=True) + 1e-05)
    scaled = widened * inv_rms
    return ((scaled * gain_row).astype(jnp.bfloat16), scaled, inv_rms)


def route_gates(normed, router_table, routes):
    logits = jnp.dot(normed, router_table, preferred_element_type=jnp.float32)
    columns = jnp.arange(router_table.shape[1], dtype=jnp.int32)
    picked = (routes[:, :, None] == columns[None, None, :]).astype(jnp.float32)
    chosen = jnp.sum(logits[:, None, :] * picked, axis=2)
    first_gate = jax.nn.sigmoid(chosen[:, 0] - chosen[:, 1])
    second = jax.nn.sigmoid(chosen[:, 1] - chosen[:, 0])
    return (jnp.stack([first_gate, second], axis=1), picked)


def slot_plan(routes, half_cap, sender):
    flat_routes = routes.reshape(-1)
    rows = jnp.arange(flat_routes.shape[0], dtype=jnp.int32)
    before = (rows[:, None] > rows[None, :]) & (flat_routes[:, None] == flat_routes[None, :])
    position = jnp.sum(before.astype(jnp.int32), axis=1)
    target = 2 * flat_routes + (position + sender) % 2
    return target * half_cap + position // 2


def pack_rows(row_block, slots, slot_total):
    blank_rows = jnp.zeros((slot_total, row_block.shape[1]), row_block.dtype)
    return blank_rows.at[slots].set(row_block)


def transposed(left, right):
    return lax.dot_general(
        left, right, (((1,), (1,)), ((), ())), preferred_element_type=jnp.float32
    )


def expert_forward(pieces, halves):
    own_up, other_up, own_down, other_down = halves
    row_block = pieces.reshape(-1, pieces.shape[-1])
    active_own = gelu_parts(jnp.dot(row_block, own_up, preferred_element_type=jnp.float32))[
        0
    ].astype(jnp.bfloat16)
    active_other = gelu_parts(jnp.dot(row_block, other_up, preferred_element_type=jnp.float32))[
        0
    ].astype(jnp.bfloat16)
    total = jnp.dot(active_own, own_down, preferred_element_type=jnp.float32) + jnp.dot(
        active_other, other_down, preferred_element_type=jnp.float32
    )
    return total.astype(jnp.bfloat16).reshape(pieces.shape)


def expert_backward(pieces, grad_pieces, halves):
    own_up, other_up, own_down, other_down = halves
    row_block = pieces.reshape(-1, pieces.shape[-1])
    grad_rows = grad_pieces.reshape(-1, pieces.shape[-1])
    active_own, slope_own = gelu_parts(
        jnp.dot(row_block, own_up, preferred_element_type=jnp.float32)
    )
    active_other, slope_other = gelu_parts(
        jnp.dot(row_block, other_up, preferred_element_type=jnp.float32)
    )
    total = jnp.dot(
        active_own.astype(jnp.bfloat16), own_down, preferred_element_type=jnp.float32
    ) + jnp.dot(active_other.astype(jnp.bfloat16), other_down, preferred_element_type=jnp.float32)
    back_own = (transposed(grad_rows, own_down) * slope_own).astype(jnp.bfloat16)
    back_other = (transposed(grad_rows, other_down) * slope_other).astype(jnp.bfloat16)
    input_grads = transposed(back_own, own_up) + transposed(back_other, other_up)
    return (
        total.astype(jnp.bfloat16).reshape(pieces.shape),
        input_grads.astype(jnp.bfloat16).reshape(pieces.shape),
    )


def dispatched(
    handoff,
    saved_in,
    grad_handoff,
    route_fwd,
    route_bwd,
    norm_gain,
    router,
    up_proj,
    down_proj,
    moment_m,
    moment_v,
):
    tok_rows = handoff.shape[1]
    feature_dim = handoff.shape[2]
    devices = lax.axis_size("expert")
    experts = devices // 2
    half_cap = max(3, 3 * tok_rows // (2 * experts))
    slot_total = devices * half_cap
    gain_row = norm_gain[0]
    router_table = router[0]
    sender = lax.axis_index("expert")
    entering = shifted(handoff[0], "pipe", 1)
    arriving = shifted(grad_handoff[0], "pipe", -1)
    own_up = up_proj[0]
    own_down = down_proj[0]
    other_up, other_down = from_partner((own_up, own_down), "expert", 0)
    halves = (own_up, other_up, own_down, other_down)
    normed_fwd = normalize(entering, gain_row)[0]
    gates_fwd = route_gates(normed_fwd, router_table, route_fwd[0])[0]
    slots_fwd = slot_plan(route_fwd[0], half_cap, sender)
    send_fwd = pack_rows(jnp.repeat(normed_fwd, 2, axis=0), slots_fwd, slot_total).reshape(
        devices, half_cap, feature_dim
    )
    normed_bwd, scaled_bwd, inv_rms = normalize(saved_in[0], gain_row)
    gates_bwd, picked = route_gates(normed_bwd, router_table, route_bwd[0])
    slots_bwd = slot_plan(route_bwd[0], half_cap, sender)
    send_bwd = pack_rows(jnp.repeat(normed_bwd, 2, axis=0), slots_bwd, slot_total).reshape(
        devices, half_cap, feature_dim
    )
    cotangent = arriving.astype(jnp.float32)
    slot_grads = (
        (gates_bwd[:, :, None] * cotangent[:, None, :])
        .astype(jnp.bfloat16)
        .reshape(-1, feature_dim)
    )
    send_grad = pack_rows(slot_grads, slots_bwd, slot_total).reshape(devices, half_cap, feature_dim)
    back_fwd = lax.all_to_all(
        expert_forward(
            lax.all_to_all(send_fwd, "expert", split_axis=0, concat_axis=0, tiled=True), halves
        ),
        "expert",
        split_axis=0,
        concat_axis=0,
        tiled=True,
    )
    out_second, grad_second = expert_backward(
        lax.all_to_all(send_bwd, "expert", split_axis=0, concat_axis=0, tiled=True),
        lax.all_to_all(send_grad, "expert", split_axis=0, concat_axis=0, tiled=True),
        halves,
    )
    back_bwd = lax.all_to_all(out_second, "expert", split_axis=0, concat_axis=0, tiled=True)
    back_grad = lax.all_to_all(grad_second, "expert", split_axis=0, concat_axis=0, tiled=True)
    out_fwd = (
        back_fwd.reshape(slot_total, feature_dim)[slots_fwd]
        .reshape(tok_rows, 2, feature_dim)
        .astype(jnp.float32)
    )
    segment_sum = (
        entering.astype(jnp.float32)
        + gates_fwd[:, 0:1] * out_fwd[:, 0]
        + gates_fwd[:, 1:2] * out_fwd[:, 1]
    )
    out_bwd = (
        back_bwd.reshape(slot_total, feature_dim)[slots_bwd]
        .reshape(tok_rows, 2, feature_dim)
        .astype(jnp.float32)
    )
    grads_in = (
        back_grad.reshape(slot_total, feature_dim)[slots_bwd]
        .reshape(tok_rows, 2, feature_dim)
        .astype(jnp.float32)
    )
    gate_grads = jnp.sum(cotangent[:, None, :] * out_bwd, axis=2)
    logit_step = gates_bwd[:, 0] * gates_bwd[:, 1] * (gate_grads[:, 0] - gate_grads[:, 1])
    logit_grads = (logit_step[:, None] * (picked[:, 0, :] - picked[:, 1, :])).astype(jnp.bfloat16)
    local_grad = lax.dot_general(
        normed_bwd, logit_grads, (((0,), (0,)), ((), ())), preferred_element_type=jnp.float32
    )
    router_back = transposed(logit_grads, router_table)
    normed_grad = grads_in[:, 0] + grads_in[:, 1] + router_back
    scaled_grad = normed_grad * gain_row
    input_grad = inv_rms * (
        scaled_grad - scaled_bwd * jnp.mean(scaled_grad * scaled_bwd, axis=-1, keepdims=True)
    )
    grad_back = (cotangent + input_grad).astype(jnp.bfloat16)
    row_count = feature_dim // devices
    summed = lax.psum(local_grad, "expert")
    norm_sq = lax.psum(jnp.sum(summed * summed), "pipe")
    grad_rows = lax.dynamic_slice_in_dim(summed, sender * row_count, row_count, 0)
    factor = jnp.minimum(1.0, clip_norm / jnp.sqrt(norm_sq))
    clipped = grad_rows * factor
    new_m = beta_first * moment_m[0] + (1.0 - beta_first) * clipped
    new_v = beta_second * moment_v[0] + (1.0 - beta_second) * clipped * clipped
    first_fix = 1.0 - beta_first**STEP
    second_fix = 1.0 - beta_second**STEP
    router_update = new_m / first_fix / (jnp.sqrt(new_v / second_fix) + 1e-08)
    return (
        segment_sum.astype(jnp.bfloat16)[None],
        grad_back[None],
        new_m[None],
        new_v[None],
        router_update[None],
    )


PIECES = 4
SLOTS = 16
MIB = 2**20


def permuted(value, axes, target):
    sizes = [lax.axis_size(axis) for axis in axes]
    count = math.prod(sizes)
    pairs = []
    for source in range(count):
        place = (source // sizes[-1], source % sizes[-1]) if len(axes) == 2 else (0, source)
        row, column = target(*place)
        pairs.append((source, (row % sizes[0]) * sizes[-1] + column if len(axes) == 2 else column))
    return lax.ppermute(value, axes if len(axes) == 2 else axes[0], pairs)


def normed_rows(block, gain_row):
    widened = block.astype(jnp.float32)
    inv_rms = lax.rsqrt(jnp.mean(widened * widened, axis=-1, keepdims=True) + 1e-05)
    return (widened * inv_rms * gain_row).astype(jnp.bfloat16)


def gates_of(rows, router_rows, routes):
    logits = lax.dot_general(
        rows, router_rows, (((1,), (1,)), ((), ())), preferred_element_type=jnp.float32
    )
    column = lax.broadcasted_iota(jnp.int32, logits.shape, 1)
    first, second = routes[:, 0:1], routes[:, 1:2]
    logit_first = jnp.sum(jnp.where(column == first, logits, 0.0), axis=1, keepdims=True)
    logit_second = jnp.sum(jnp.where(column == second, logits, 0.0), axis=1, keepdims=True)
    gate_first = jax.nn.sigmoid(logit_first - logit_second)
    gate_second = jax.nn.sigmoid(logit_second - logit_first)
    return first, second, gate_first, gate_second


def route_columns(marks, row):
    turned = jnp.concatenate([marks[0], marks[1]], axis=1).astype(jnp.float32).T
    picked = turned[:, row : row + 2].astype(jnp.int32)
    return picked


def start_weights(pieces, up_all, down_all, arrived):
    width = up_all.shape[0] // PIECES
    ups, downs = [], []
    for i in range(PIECES):
        part = pl.ds(i * width, width)
        ups.append(
            pltpu.make_async_copy(pieces[i].at[pl.ds(0, width)], up_all.at[part], arrived.at[i])
        )
        downs.append(
            pltpu.make_async_copy(
                pieces[i].at[pl.ds(width, width)], down_all.at[part], arrived.at[PIECES + i]
            )
        )
    for i in range(PIECES):
        ups[i].start()
        downs[i].start()
    return width, ups, downs


def pick(first, second, for_first, for_second, expert):
    return jnp.where(first == expert, for_first, 0.0) + jnp.where(
        second == expert, for_second, 0.0
    )


def forward_kernel(held, next_here, next_there, listed, marked, gain, router_rows, *rest):
    pieces = rest[:PIECES]
    kept, sent, up_all, down_all, entered, rows, hidden, marks, arrived, landed = rest[PIECES:]
    tokens = next_here.shape[0]
    lines, lanes = pl.ds(tokens, SLOTS), pl.ds(0, tokens)
    loads = [
        pltpu.make_async_copy(next_here, entered.at[pl.ds(0, tokens)], landed.at[0]),
        pltpu.make_async_copy(next_there.at[pl.ds(0, tokens)], entered.at[pl.ds(tokens, tokens)], landed.at[1]),
        pltpu.make_async_copy(listed.at[:, lanes], marks.at[0], landed.at[2]),
        pltpu.make_async_copy(marked.at[lines, lanes], marks.at[1], landed.at[3]),
    ]
    for load in loads:
        load.start()
    width, ups, downs = start_weights(pieces, up_all, down_all, arrived)
    for load in loads:
        load.wait()
    routes = route_columns(marks, 0)
    rows[...] = normed_rows(entered[...], gain[...])
    first, second, gate_first, gate_second = gates_of(rows[...], router_rows[...], routes)
    for i in range(PIECES):
        part = slice(i * width, (i + 1) * width)
        ups[i].wait()
        preact = transposed(rows[...], up_all[part, :])
        gate = pick(first, second, gate_first, gate_second, held[2 * i // PIECES])
        hidden[:, part] = (gelu_parts(preact)[0] * gate).astype(jnp.bfloat16)
    for down in downs:
        down.wait()
    block = 512
    for start in range(0, kept.shape[1], block):
        part = slice(start, start + block)
        total = jnp.dot(hidden[...], down_all[:, part], preferred_element_type=jnp.float32)
        kept[:, part] = entered[:tokens, part].astype(jnp.float32) + total[:tokens]
        sent[:, part] = total[tokens:].astype(jnp.bfloat16)


def backward_kernel(
    held, saved_here, saved_there, grad_here, grad_there, listed, marked, gain, router_rows, *rest
):
    pieces = rest[:PIECES]
    (
        kept,
        sent,
        up_all,
        down_all,
        saved,
        grads,
        rows,
        backs,
        marks,
        arrived,
        landed,
    ) = rest[PIECES:]
    tokens = saved_here.shape[0]
    lines, lanes = pl.ds(tokens, SLOTS), pl.ds(0, tokens)
    upper, lower = pl.ds(0, tokens), pl.ds(tokens, tokens)
    loads = [
        pltpu.make_async_copy(saved_here, saved.at[upper], landed.at[0]),
        pltpu.make_async_copy(saved_there, saved.at[lower], landed.at[1]),
        pltpu.make_async_copy(grad_here, grads.at[upper], landed.at[2]),
        pltpu.make_async_copy(grad_there, grads.at[lower], landed.at[3]),
        pltpu.make_async_copy(listed.at[:, lanes], marks.at[0], landed.at[4]),
        pltpu.make_async_copy(marked.at[lines, lanes], marks.at[1], landed.at[5]),
    ]
    for load in loads:
        load.start()
    width, ups, downs = start_weights(pieces, up_all, down_all, arrived)
    for load in loads:
        load.wait()
    routes = route_columns(marks, 2)
    rows[...] = normed_rows(saved[...], gain[...])
    first, second, gate_first, gate_second = gates_of(rows[...], router_rows[...], routes)
    signed_sum = jnp.zeros_like(gate_first)
    for i in range(PIECES):
        expert = held[2 * i // PIECES]
        part = slice(i * width, (i + 1) * width)
        ups[i].wait()
        preact = transposed(rows[...], up_all[part, :])
        downs[i].wait()
        hidden_grad = transposed(grads[...], down_all[part, :])
        active, slope = gelu_parts(preact)
        active = active.astype(jnp.bfloat16).astype(jnp.float32)
        signed_sum += pick(first, second, 1.0, -1.0, expert) * jnp.sum(
            active * hidden_grad, axis=1, keepdims=True
        )
        gate = pick(first, second, gate_first, gate_second, expert)
        backs[:, part] = (hidden_grad * slope * gate).astype(jnp.bfloat16)
    step = gate_first * gate_second * signed_sum
    column = lax.broadcasted_iota(jnp.int32, (2 * tokens, SLOTS), 1)
    expert = jnp.where(column < SLOTS // 4, column, column - SLOTS // 4)
    step = pick(first, second, step, -step, expert)
    coarse = step.astype(jnp.bfloat16).astype(jnp.float32)
    logit_grads = jnp.where(column < SLOTS // 4, coarse, step - coarse)
    logit_grads = jnp.where(column < SLOTS // 2, logit_grads, 0.0).astype(jnp.bfloat16)
    block = 512
    for start in range(0, kept.shape[1], block):
        part = slice(start, start + block)
        parts = lax.dot_general(
            logit_grads,
            rows[:, part],
            (((0,), (0,)), ((), ())),
            preferred_element_type=jnp.float32,
        )
        parts = parts + pltpu.roll(parts, SLOTS - SLOTS // 4, 0)
        high = parts.astype(jnp.bfloat16).astype(jnp.float32)
        low = pltpu.roll(parts - high, SLOTS // 4, 0)
        row = lax.broadcasted_iota(jnp.int32, parts.shape, 0)
        sent[tokens : tokens + SLOTS, part] = jnp.where(
            row < SLOTS // 4, high, low
        ).astype(jnp.bfloat16)
        total = jnp.dot(
            backs[...], up_all[:, part], preferred_element_type=jnp.float32
        ) + jnp.dot(logit_grads, router_rows[:, part], preferred_element_type=jnp.float32)
        kept[:, part] = total[:tokens]
        sent[:tokens, part] = total[tokens:].astype(jnp.bfloat16)


def closing_kernel(saved, arriving, gain, kept, came, out):
    widened = saved[...].astype(jnp.float32)
    inv_rms = lax.rsqrt(jnp.mean(widened * widened, axis=-1, keepdims=True) + 1e-05)
    scaled = widened * inv_rms
    scaled_grad = (kept[...] + came[...].astype(jnp.float32)) * gain[...]
    mean = jnp.mean(scaled_grad * scaled, axis=-1, keepdims=True)
    input_grad = inv_rms * (scaled_grad - scaled * mean)
    out[...] = (arriving[...].astype(jnp.float32) + input_grad).astype(jnp.bfloat16)


def in_hbm(count):
    return [pl.BlockSpec(memory_space=pltpu.HBM)] * count


def in_vmem(count):
    return [pl.BlockSpec(memory_space=pltpu.VMEM)] * count


def run_experts(kernel, held, blocks, lists, gain, router_rows, pieces, matmuls, more_rows):
    tokens, features = blocks[0].shape
    hidden = PIECES * pieces[0].shape[0] // 2
    weights = pltpu.VMEM((hidden, features), jnp.bfloat16)
    rows = pltpu.VMEM((2 * tokens, features), jnp.bfloat16)
    return pl.pallas_call(
        kernel,
        out_shape=(
            jax.ShapeDtypeStruct((tokens, features), jnp.float32),
            jax.ShapeDtypeStruct((tokens + more_rows, features), jnp.bfloat16),
        ),
        in_specs=[pl.BlockSpec(memory_space=pltpu.SMEM)]
        + in_hbm(len(blocks) + 2)
        + in_vmem(2)
        + in_hbm(PIECES),
        out_specs=tuple(in_vmem(2)),
        scratch_shapes=[
            weights,
            weights,
            *[rows] * (len(blocks) // 2 + 1),
            pltpu.VMEM((2 * tokens, hidden), jnp.bfloat16),
            pltpu.VMEM((2, SLOTS, tokens), jnp.bfloat16),
            pltpu.SemaphoreType.DMA((2 * PIECES,)),
            pltpu.SemaphoreType.DMA((len(blocks) + 2,)),
        ],
        compiler_params=pltpu.CompilerParams(vmem_limit_bytes=60 * MIB),
        cost_estimate=pl.CostEstimate(
            flops=4 * matmuls * tokens * features * hidden,
            bytes_accessed=4 * features * hidden + 16 * tokens * features,
            transcendentals=2 * tokens * hidden,
        ),
    )(held, *blocks, *lists, gain, router_rows, *pieces)


def run_closing(saved, arriving, gain, kept, came):
    tokens, features = saved.shape
    block = tokens // 4
    rows = pl.BlockSpec((block, features), lambda i: (i, 0))
    return pl.pallas_call(
        closing_kernel,
        out_shape=jax.ShapeDtypeStruct((tokens, features), jnp.bfloat16),
        grid=(4,),
        in_specs=[
            rows,
            rows,
            pl.BlockSpec((1, features), lambda i: (0, 0)),
            rows,
            rows,
        ],
        out_specs=rows,
        cost_estimate=pl.CostEstimate(
            flops=16 * tokens * features, bytes_accessed=12 * tokens * features, transcendentals=0
        ),
    )(saved, arriving, gain, kept, came)


def after(value, *earlier):
    return lax.optimization_barrier((value, *earlier))[0]


def paired(
    handoff,
    saved_in,
    grad_handoff,
    route_fwd,
    route_bwd,
    norm_gain,
    router,
    up_proj,
    down_proj,
    moment_m,
    moment_v,
):
    def shift(value, by):
        return permuted(value, both, lambda row, place: (row + by, place))

    def mirror(value, by=0):
        if by == 0:
            return permuted(value, line, lambda row, place: (row, place ^ 6))
        return permuted(value, both, lambda row, place: (row + by, place ^ 6))

    def near(value):
        return permuted(value, line, lambda row, place: (row, place ^ 2))

    def across(value):
        return permuted(value, line, lambda row, place: (row, place ^ 1))

    both, line = ("pipe", "expert"), ("expert",)
    sender = lax.axis_index("expert")
    saved, leaving, cotangent = saved_in[0], handoff[0], grad_handoff[0]
    routes = jnp.concatenate([route_fwd[0].T, route_bwd[0].T], axis=0)
    tokens, features = saved.shape
    listed = jnp.pad(
        routes.astype(jnp.bfloat16), ((0, SLOTS - routes.shape[0]), (0, features - tokens))
    )
    saved_there = mirror(saved)
    entering = shift(leaving, 1)
    arriving = shift(after(cotangent, entering), -1)
    own = jnp.concatenate([up_proj[0].T, down_proj[0]], axis=0)
    close = near(own)
    own_other = across(own)
    chip = sender // 2
    held = jnp.stack([chip, chip ^ 1]).astype(jnp.int32)
    router_turned = router[0].T
    router_rows = jnp.concatenate(
        [router_turned, router_turned, jnp.zeros((SLOTS // 2, router_turned.shape[1]), jnp.bfloat16)]
    )
    arriving_there = mirror(after(arriving, own_other, saved_there, held, router_rows))
    entering_there = mirror(jnp.concatenate([entering, listed], axis=0), 0)
    close_other = across(after(close, arriving_there, entering_there))
    pieces = (own, own_other, close, close_other)
    quarter = SLOTS // 4
    kept_bwd, sent_bwd = run_experts(
        backward_kernel,
        held,
        (saved, saved_there, arriving, arriving_there),
        (listed, entering_there),
        norm_gain,
        router_rows,
        pieces,
        3,
        SLOTS,
    )
    came_bwd = mirror(sent_bwd)
    kept_fwd, sent_fwd = run_experts(
        forward_kernel,
        held,
        (entering, after(entering_there, sent_bwd)),
        (listed, entering_there),
        norm_gain,
        router_rows,
        pieces,
        2,
        0,
    )
    came_fwd = mirror(sent_fwd)
    grad_back = run_closing(saved, arriving, norm_gain, kept_bwd, came_bwd)
    terms = sent_bwd[tokens:].astype(jnp.float32) + came_bwd[tokens:].astype(jnp.float32)
    terms = terms[:quarter] + terms[quarter : 2 * quarter]
    devices = lax.axis_size("expert")
    four = devices // 2
    terms = jnp.broadcast_to(terms[None], (four, *terms.shape))
    groups = [[first * four + i for i in range(four)] for first in range(2)]
    terms = lax.all_to_all(
        terms, "expert", split_axis=0, concat_axis=0, tiled=True, axis_index_groups=groups
    )
    summed = jnp.sum(terms, axis=0)
    square = jnp.sum(summed * summed, keepdims=True)
    square = after(jnp.broadcast_to(square, (1, 128)), grad_back)
    total = square
    for by in range(1, lax.axis_size("pipe")):
        total += shift(square, by)
    norm_sq = total[0, 0]
    width = summed.shape[1] // devices
    grad_rows = lax.dynamic_slice_in_dim(summed, sender * width, width, 1).T
    factor = jnp.minimum(1.0, clip_norm / jnp.sqrt(norm_sq))
    clipped = grad_rows * factor
    new_m = beta_first * moment_m[0] + (1.0 - beta_first) * clipped
    new_v = beta_second * moment_v[0] + (1.0 - beta_second) * clipped * clipped
    first_fix = 1.0 - beta_first**STEP
    second_fix = 1.0 - beta_second**STEP
    router_update = new_m / first_fix / (jnp.sqrt(new_v / second_fix) + 1e-08)
    segment_out = (kept_fwd + came_fwd.astype(jnp.float32)).astype(jnp.bfloat16)
    return (
        segment_out[None],
        grad_back[None],
        new_m[None],
        new_v[None],
        router_update[None],
    )


def solution(mesh):
    in_specs = (
        P("pipe", "expert", None),
        P("pipe", "expert", None),
        P("pipe", "expert", None),
        P("pipe", "expert", None),
        P("pipe", "expert", None),
        P("pipe", None),
        P("pipe", None, None),
        P("pipe", None, "expert"),
        P("pipe", "expert", None),
        P("pipe", "expert", None),
        P("pipe", "expert", None),
    )
    out_specs = (
        P("pipe", "expert", None),
        P("pipe", "expert", None),
        P("pipe", "expert", None),
        P("pipe", "expert", None),
        P("pipe", "expert", None),
    )
    experts_held = mesh.shape["expert"] // 2
    return jax.shard_map(
        paired if experts_held == 4 else dispatched, mesh=mesh, in_specs=in_specs, out_specs=out_specs, check_vma=False
    )
```

```python
import math

import jax
import jax.numpy as jnp
from jax import lax
from jax.experimental import pallas as pl
from jax.experimental.pallas import tpu as pltpu
from jax.sharding import PartitionSpec as P

STEP = 10


gelu_scale = math.sqrt(2.0 / math.pi)
beta_first = 0.9
beta_second = 0.95
clip_norm = 1.0


def shifted(x, axis, by):
    length = lax.axis_size(axis)
    return lax.ppermute(x, axis, [(i, (i + by) % length) for i in range(length)])


def from_partner(value, axis, bit):
    mask = 2**bit
    pairs = [(source, source ^ mask) for source in range(lax.axis_size(axis))]
    return lax.ppermute(value, axis, pairs)


def gelu_parts(preact):
    square = preact * preact
    tangent = jnp.tanh(gelu_scale * (preact + 0.044715 * square * preact))
    activated = 0.5 * preact * (1.0 + tangent)
    gelu_slope = 0.5 * (1.0 + tangent) + 0.5 * preact * (1.0 - tangent * tangent) * gelu_scale * (
        1.0 + 0.134145 * square
    )
    return (activated, gelu_slope)


def normalize(inputs, gain_row):
    widened = inputs.astype(jnp.float32)
    inv_rms = lax.rsqrt(jnp.mean(widened * widened, axis=-1, keepdims=True) + 1e-05)
    scaled = widened * inv_rms
    return ((scaled * gain_row).astype(jnp.bfloat16), scaled, inv_rms)


def route_gates(normed, router_table, routes):
    logits = jnp.dot(normed, router_table, preferred_element_type=jnp.float32)
    columns = jnp.arange(router_table.shape[1], dtype=jnp.int32)
    picked = (routes[:, :, None] == columns[None, None, :]).astype(jnp.float32)
    chosen = jnp.sum(logits[:, None, :] * picked, axis=2)
    first_gate = jax.nn.sigmoid(chosen[:, 0] - chosen[:, 1])
    second = jax.nn.sigmoid(chosen[:, 1] - chosen[:, 0])
    return (jnp.stack([first_gate, second], axis=1), picked)


def slot_plan(routes, half_cap, sender):
    flat_routes = routes.reshape(-1)
    rows = jnp.arange(flat_routes.shape[0], dtype=jnp.int32)
    before = (rows[:, None] > rows[None, :]) & (flat_routes[:, None] == flat_routes[None, :])
    position = jnp.sum(before.astype(jnp.int32), axis=1)
    target = 2 * flat_routes + (position + sender) % 2
    return target * half_cap + position // 2


def pack_rows(row_block, slots, slot_total):
    blank_rows = jnp.zeros((slot_total, row_block.shape[1]), row_block.dtype)
    return blank_rows.at[slots].set(row_block)


def transposed(left, right):
    return lax.dot_general(
        left, right, (((1,), (1,)), ((), ())), preferred_element_type=jnp.float32
    )


def expert_forward(pieces, halves):
    own_up, other_up, own_down, other_down = halves
    row_block = pieces.reshape(-1, pieces.shape[-1])
    active_own = gelu_parts(jnp.dot(row_block, own_up, preferred_element_type=jnp.float32))[
        0
    ].astype(jnp.bfloat16)
    active_other = gelu_parts(jnp.dot(row_block, other_up, preferred_element_type=jnp.float32))[
        0
    ].astype(jnp.bfloat16)
    total = jnp.dot(active_own, own_down, preferred_element_type=jnp.float32) + jnp.dot(
        active_other, other_down, preferred_element_type=jnp.float32
    )
    return total.astype(jnp.bfloat16).reshape(pieces.shape)


def expert_backward(pieces, grad_pieces, halves):
    own_up, other_up, own_down, other_down = halves
    row_block = pieces.reshape(-1, pieces.shape[-1])
    grad_rows = grad_pieces.reshape(-1, pieces.shape[-1])
    active_own, slope_own = gelu_parts(
        jnp.dot(row_block, own_up, preferred_element_type=jnp.float32)
    )
    active_other, slope_other = gelu_parts(
        jnp.dot(row_block, other_up, preferred_element_type=jnp.float32)
    )
    total = jnp.dot(
        active_own.astype(jnp.bfloat16), own_down, preferred_element_type=jnp.float32
    ) + jnp.dot(active_other.astype(jnp.bfloat16), other_down, preferred_element_type=jnp.float32)
    back_own = (transposed(grad_rows, own_down) * slope_own).astype(jnp.bfloat16)
    back_other = (transposed(grad_rows, other_down) * slope_other).astype(jnp.bfloat16)
    input_grads = transposed(back_own, own_up) + transposed(back_other, other_up)
    return (
        total.astype(jnp.bfloat16).reshape(pieces.shape),
        input_grads.astype(jnp.bfloat16).reshape(pieces.shape),
    )


def dispatched(
    handoff,
    saved_in,
    grad_handoff,
    route_fwd,
    route_bwd,
    norm_gain,
    router,
    up_proj,
    down_proj,
    moment_m,
    moment_v,
):
    tok_rows = handoff.shape[1]
    feature_dim = handoff.shape[2]
    devices = lax.axis_size("expert")
    experts = devices // 2
    half_cap = max(3, 3 * tok_rows // (2 * experts))
    slot_total = devices * half_cap
    gain_row = norm_gain[0]
    router_table = router[0]
    sender = lax.axis_index("expert")
    entering = shifted(handoff[0], "pipe", 1)
    arriving = shifted(grad_handoff[0], "pipe", -1)
    own_up = up_proj[0]
    own_down = down_proj[0]
    other_up, other_down = from_partner((own_up, own_down), "expert", 0)
    halves = (own_up, other_up, own_down, other_down)
    normed_fwd = normalize(entering, gain_row)[0]
    gates_fwd = route_gates(normed_fwd, router_table, route_fwd[0])[0]
    slots_fwd = slot_plan(route_fwd[0], half_cap, sender)
    send_fwd = pack_rows(jnp.repeat(normed_fwd, 2, axis=0), slots_fwd, slot_total).reshape(
        devices, half_cap, feature_dim
    )
    normed_bwd, scaled_bwd, inv_rms = normalize(saved_in[0], gain_row)
    gates_bwd, picked = route_gates(normed_bwd, router_table, route_bwd[0])
    slots_bwd = slot_plan(route_bwd[0], half_cap, sender)
    send_bwd = pack_rows(jnp.repeat(normed_bwd, 2, axis=0), slots_bwd, slot_total).reshape(
        devices, half_cap, feature_dim
    )
    cotangent = arriving.astype(jnp.float32)
    slot_grads = (
        (gates_bwd[:, :, None] * cotangent[:, None, :])
        .astype(jnp.bfloat16)
        .reshape(-1, feature_dim)
    )
    send_grad = pack_rows(slot_grads, slots_bwd, slot_total).reshape(devices, half_cap, feature_dim)
    back_fwd = lax.all_to_all(
        expert_forward(
            lax.all_to_all(send_fwd, "expert", split_axis=0, concat_axis=0, tiled=True), halves
        ),
        "expert",
        split_axis=0,
        concat_axis=0,
        tiled=True,
    )
    out_second, grad_second = expert_backward(
        lax.all_to_all(send_bwd, "expert", split_axis=0, concat_axis=0, tiled=True),
        lax.all_to_all(send_grad, "expert", split_axis=0, concat_axis=0, tiled=True),
        halves,
    )
    back_bwd = lax.all_to_all(out_second, "expert", split_axis=0, concat_axis=0, tiled=True)
    back_grad = lax.all_to_all(grad_second, "expert", split_axis=0, concat_axis=0, tiled=True)
    out_fwd = (
        back_fwd.reshape(slot_total, feature_dim)[slots_fwd]
        .reshape(tok_rows, 2, feature_dim)
        .astype(jnp.float32)
    )
    segment_sum = (
        entering.astype(jnp.float32)
        + gates_fwd[:, 0:1] * out_fwd[:, 0]
        + gates_fwd[:, 1:2] * out_fwd[:, 1]
    )
    out_bwd = (
        back_bwd.reshape(slot_total, feature_dim)[slots_bwd]
        .reshape(tok_rows, 2, feature_dim)
        .astype(jnp.float32)
    )
    grads_in = (
        back_grad.reshape(slot_total, feature_dim)[slots_bwd]
        .reshape(tok_rows, 2, feature_dim)
        .astype(jnp.float32)
    )
    gate_grads = jnp.sum(cotangent[:, None, :] * out_bwd, axis=2)
    logit_step = gates_bwd[:, 0] * gates_bwd[:, 1] * (gate_grads[:, 0] - gate_grads[:, 1])
    logit_grads = (logit_step[:, None] * (picked[:, 0, :] - picked[:, 1, :])).astype(jnp.bfloat16)
    local_grad = lax.dot_general(
        normed_bwd, logit_grads, (((0,), (0,)), ((), ())), preferred_element_type=jnp.float32
    )
    router_back = transposed(logit_grads, router_table)
    normed_grad = grads_in[:, 0] + grads_in[:, 1] + router_back
    scaled_grad = normed_grad * gain_row
    input_grad = inv_rms * (
        scaled_grad - scaled_bwd * jnp.mean(scaled_grad * scaled_bwd, axis=-1, keepdims=True)
    )
    grad_back = (cotangent + input_grad).astype(jnp.bfloat16)
    row_count = feature_dim // devices
    summed = lax.psum(local_grad, "expert")
    norm_sq = lax.psum(jnp.sum(summed * summed), "pipe")
    grad_rows = lax.dynamic_slice_in_dim(summed, sender * row_count, row_count, 0)
    factor = jnp.minimum(1.0, clip_norm / jnp.sqrt(norm_sq))
    clipped = grad_rows * factor
    new_m = beta_first * moment_m[0] + (1.0 - beta_first) * clipped
    new_v = beta_second * moment_v[0] + (1.0 - beta_second) * clipped * clipped
    first_fix = 1.0 - beta_first**STEP
    second_fix = 1.0 - beta_second**STEP
    router_update = new_m / first_fix / (jnp.sqrt(new_v / second_fix) + 1e-08)
    return (
        segment_sum.astype(jnp.bfloat16)[None],
        grad_back[None],
        new_m[None],
        new_v[None],
        router_update[None],
    )


PIECES = 4
SLOTS = 16
MIB = 2**20


def permuted(value, axes, target):
    sizes = [lax.axis_size(axis) for axis in axes]
    count = math.prod(sizes)
    pairs = []
    for source in range(count):
        place = (source // sizes[-1], source % sizes[-1]) if len(axes) == 2 else (0, source)
        row, column = target(*place)
        pairs.append((source, (row % sizes[0]) * sizes[-1] + column if len(axes) == 2 else column))
    return lax.ppermute(value, axes if len(axes) == 2 else axes[0], pairs)


def normed_rows(block, gain_row):
    widened = block.astype(jnp.float32)
    inv_rms = lax.rsqrt(jnp.mean(widened * widened, axis=-1, keepdims=True) + 1e-05)
    return (widened * inv_rms * gain_row).astype(jnp.bfloat16)


def gates_of(rows, router_rows, routes):
    logits = lax.dot_general(
        rows, router_rows, (((1,), (1,)), ((), ())), preferred_element_type=jnp.float32
    )
    column = lax.broadcasted_iota(jnp.int32, logits.shape, 1)
    first, second = routes[:, 0:1], routes[:, 1:2]
    logit_first = jnp.sum(jnp.where(column == first, logits, 0.0), axis=1, keepdims=True)
    logit_second = jnp.sum(jnp.where(column == second, logits, 0.0), axis=1, keepdims=True)
    gate_first = jax.nn.sigmoid(logit_first - logit_second)
    gate_second = jax.nn.sigmoid(logit_second - logit_first)
    return first, second, gate_first, gate_second


def route_columns(marks, row):
    turned = jnp.concatenate([marks[0], marks[1]], axis=1).astype(jnp.float32).T
    picked = turned[:, row : row + 2].astype(jnp.int32)
    return picked


def weight_loads(pieces, up_all, down_all, arrived):
    width = up_all.shape[0] // PIECES
    ups, downs = [], []
    for i in range(PIECES):
        part = pl.ds(i * width, width)
        ups.append(
            pltpu.make_async_copy(pieces[i].at[pl.ds(0, width)], up_all.at[part], arrived.at[i])
        )
        downs.append(
            pltpu.make_async_copy(
                pieces[i].at[pl.ds(width, width)], down_all.at[part], arrived.at[PIECES + i]
            )
        )
    return width, ups, downs


def pick(first, second, for_first, for_second, expert):
    return jnp.where(first == expert, for_first, 0.0) + jnp.where(
        second == expert, for_second, 0.0
    )


def forward_kernel(held, next_here, next_there, listed, marked, gain, router_rows, *rest):
    pieces = rest[:PIECES]
    kept, sent, up_all, down_all, entered, rows, hidden, marks, arrived, landed = rest[PIECES:]
    tokens = next_here.shape[0]
    lines, lanes = pl.ds(tokens, SLOTS), pl.ds(0, tokens)
    loads = [
        pltpu.make_async_copy(next_here, entered.at[pl.ds(0, tokens)], landed.at[0]),
        pltpu.make_async_copy(next_there.at[pl.ds(0, tokens)], entered.at[pl.ds(tokens, tokens)], landed.at[1]),
        pltpu.make_async_copy(listed.at[:, lanes], marks.at[0], landed.at[2]),
        pltpu.make_async_copy(marked.at[lines, lanes], marks.at[1], landed.at[3]),
    ]
    for load in loads:
        load.start()
    width, ups, downs = weight_loads(pieces, up_all, down_all, arrived)
    ups[0].start()
    for load in loads:
        load.wait()
    ups[1].start()
    ups[2].start()
    routes = route_columns(marks, 0)
    rows[...] = normed_rows(entered[...], gain[...])
    first, second, gate_first, gate_second = gates_of(rows[...], router_rows[...], routes)
    for i in range(PIECES):
        part = slice(i * width, (i + 1) * width)
        ups[i].wait()
        if i == 0:
            ups[PIECES - 1].start()
        downs[i].start()
        preact = transposed(rows[...], up_all[part, :])
        gate = pick(first, second, gate_first, gate_second, held[2 * i // PIECES])
        hidden[:, part] = (gelu_parts(preact)[0] * gate).astype(jnp.bfloat16)
    for down in downs:
        down.wait()
    block = 512
    for start in range(0, kept.shape[1], block):
        part = slice(start, start + block)
        total = jnp.dot(hidden[...], down_all[:, part], preferred_element_type=jnp.float32)
        kept[:, part] = entered[:tokens, part].astype(jnp.float32) + total[:tokens]
        sent[:, part] = total[tokens:].astype(jnp.bfloat16)


def backward_kernel(
    held, saved_here, saved_there, grad_here, grad_there, listed, marked, gain, router_rows, *rest
):
    pieces = rest[:PIECES]
    (
        kept,
        sent,
        up_all,
        down_all,
        saved,
        grads,
        rows,
        backs,
        marks,
        arrived,
        landed,
    ) = rest[PIECES:]
    tokens = saved_here.shape[0]
    lines, lanes = pl.ds(tokens, SLOTS), pl.ds(0, tokens)
    upper, lower = pl.ds(0, tokens), pl.ds(tokens, tokens)
    loads = [
        pltpu.make_async_copy(saved_here, saved.at[upper], landed.at[0]),
        pltpu.make_async_copy(saved_there, saved.at[lower], landed.at[1]),
        pltpu.make_async_copy(grad_here, grads.at[upper], landed.at[2]),
        pltpu.make_async_copy(grad_there, grads.at[lower], landed.at[3]),
        pltpu.make_async_copy(listed.at[:, lanes], marks.at[0], landed.at[4]),
        pltpu.make_async_copy(marked.at[lines, lanes], marks.at[1], landed.at[5]),
    ]
    early, late = loads[:2] + loads[4:], loads[2:4]
    for load in early:
        load.start()
    width, ups, downs = weight_loads(pieces, up_all, down_all, arrived)
    ups[0].start()
    for load in early:
        load.wait()
    for load in late:
        load.start()
    downs[0].start()
    ups[1].start()
    routes = route_columns(marks, 2)
    rows[...] = normed_rows(saved[...], gain[...])
    first, second, gate_first, gate_second = gates_of(rows[...], router_rows[...], routes)
    signed_sum = jnp.zeros_like(gate_first)
    for i in range(PIECES):
        expert = held[2 * i // PIECES]
        part = slice(i * width, (i + 1) * width)
        ups[i].wait()
        preact = transposed(rows[...], up_all[part, :])
        if i == 0:
            for load in late:
                load.wait()
        downs[i].wait()
        if i + 1 < PIECES:
            downs[i + 1].start()
        if i + 2 < PIECES:
            ups[i + 2].start()
        hidden_grad = transposed(grads[...], down_all[part, :])
        active, slope = gelu_parts(preact)
        active = active.astype(jnp.bfloat16).astype(jnp.float32)
        signed_sum += pick(first, second, 1.0, -1.0, expert) * jnp.sum(
            active * hidden_grad, axis=1, keepdims=True
        )
        gate = pick(first, second, gate_first, gate_second, expert)
        backs[:, part] = (hidden_grad * slope * gate).astype(jnp.bfloat16)
    step = gate_first * gate_second * signed_sum
    column = lax.broadcasted_iota(jnp.int32, (2 * tokens, SLOTS), 1)
    expert = jnp.where(column < SLOTS // 4, column, column - SLOTS // 4)
    step = pick(first, second, step, -step, expert)
    coarse = step.astype(jnp.bfloat16).astype(jnp.float32)
    logit_grads = jnp.where(column < SLOTS // 4, coarse, step - coarse)
    logit_grads = jnp.where(column < SLOTS // 2, logit_grads, 0.0).astype(jnp.bfloat16)
    block = 512
    for start in range(0, kept.shape[1], block):
        part = slice(start, start + block)
        parts = lax.dot_general(
            logit_grads,
            rows[:, part],
            (((0,), (0,)), ((), ())),
            preferred_element_type=jnp.float32,
        )
        parts = parts + pltpu.roll(parts, SLOTS - SLOTS // 4, 0)
        high = parts.astype(jnp.bfloat16).astype(jnp.float32)
        low = pltpu.roll(parts - high, SLOTS // 4, 0)
        row = lax.broadcasted_iota(jnp.int32, parts.shape, 0)
        sent[tokens : tokens + SLOTS, part] = jnp.where(
            row < SLOTS // 4, high, low
        ).astype(jnp.bfloat16)
        total = jnp.dot(
            backs[...], up_all[:, part], preferred_element_type=jnp.float32
        ) + jnp.dot(logit_grads, router_rows[:, part], preferred_element_type=jnp.float32)
        kept[:, part] = total[:tokens]
        sent[:tokens, part] = total[tokens:].astype(jnp.bfloat16)


def closing_kernel(saved, arriving, gain, kept, came, out):
    widened = saved[...].astype(jnp.float32)
    inv_rms = lax.rsqrt(jnp.mean(widened * widened, axis=-1, keepdims=True) + 1e-05)
    scaled = widened * inv_rms
    scaled_grad = (kept[...] + came[...].astype(jnp.float32)) * gain[...]
    mean = jnp.mean(scaled_grad * scaled, axis=-1, keepdims=True)
    input_grad = inv_rms * (scaled_grad - scaled * mean)
    out[...] = (arriving[...].astype(jnp.float32) + input_grad).astype(jnp.bfloat16)


def in_hbm(count):
    return [pl.BlockSpec(memory_space=pltpu.HBM)] * count


def in_vmem(count):
    return [pl.BlockSpec(memory_space=pltpu.VMEM)] * count


def run_experts(kernel, held, blocks, lists, gain, router_rows, pieces, matmuls, more_rows):
    tokens, features = blocks[0].shape
    hidden = PIECES * pieces[0].shape[0] // 2
    weights = pltpu.VMEM((hidden, features), jnp.bfloat16)
    rows = pltpu.VMEM((2 * tokens, features), jnp.bfloat16)
    return pl.pallas_call(
        kernel,
        out_shape=(
            jax.ShapeDtypeStruct((tokens, features), jnp.float32),
            jax.ShapeDtypeStruct((tokens + more_rows, features), jnp.bfloat16),
        ),
        in_specs=[pl.BlockSpec(memory_space=pltpu.SMEM)]
        + in_hbm(len(blocks) + 2)
        + in_vmem(2)
        + in_hbm(PIECES),
        out_specs=tuple(in_vmem(2)),
        scratch_shapes=[
            weights,
            weights,
            *[rows] * (len(blocks) // 2 + 1),
            pltpu.VMEM((2 * tokens, hidden), jnp.bfloat16),
            pltpu.VMEM((2, SLOTS, tokens), jnp.bfloat16),
            pltpu.SemaphoreType.DMA((2 * PIECES,)),
            pltpu.SemaphoreType.DMA((len(blocks) + 2,)),
        ],
        compiler_params=pltpu.CompilerParams(vmem_limit_bytes=60 * MIB),
        cost_estimate=pl.CostEstimate(
            flops=4 * matmuls * tokens * features * hidden,
            bytes_accessed=4 * features * hidden + 16 * tokens * features,
            transcendentals=2 * tokens * hidden,
        ),
    )(held, *blocks, *lists, gain, router_rows, *pieces)


def run_closing(saved, arriving, gain, kept, came):
    tokens, features = saved.shape
    block = tokens // 4
    rows = pl.BlockSpec((block, features), lambda i: (i, 0))
    return pl.pallas_call(
        closing_kernel,
        out_shape=jax.ShapeDtypeStruct((tokens, features), jnp.bfloat16),
        grid=(4,),
        in_specs=[
            rows,
            rows,
            pl.BlockSpec((1, features), lambda i: (0, 0)),
            rows,
            rows,
        ],
        out_specs=rows,
        cost_estimate=pl.CostEstimate(
            flops=16 * tokens * features, bytes_accessed=12 * tokens * features, transcendentals=0
        ),
    )(saved, arriving, gain, kept, came)


def after(value, *earlier):
    return lax.optimization_barrier((value, *earlier))[0]


def paired(
    handoff,
    saved_in,
    grad_handoff,
    route_fwd,
    route_bwd,
    norm_gain,
    router,
    up_proj,
    down_proj,
    moment_m,
    moment_v,
):
    def shift(value, by):
        return permuted(value, both, lambda row, place: (row + by, place))

    def mirror(value, by=0):
        if by == 0:
            return permuted(value, line, lambda row, place: (row, place ^ 6))
        return permuted(value, both, lambda row, place: (row + by, place ^ 6))

    def near(value):
        return permuted(value, line, lambda row, place: (row, place ^ 2))

    def across(value):
        return permuted(value, line, lambda row, place: (row, place ^ 1))

    both, line = ("pipe", "expert"), ("expert",)
    sender = lax.axis_index("expert")
    saved, leaving, cotangent = saved_in[0], handoff[0], grad_handoff[0]
    routes = jnp.concatenate([route_fwd[0].T, route_bwd[0].T], axis=0)
    tokens, features = saved.shape
    listed = jnp.pad(
        routes.astype(jnp.bfloat16), ((0, SLOTS - routes.shape[0]), (0, features - tokens))
    )
    saved_there = mirror(saved)
    entering = shift(leaving, 1)
    arriving = shift(after(cotangent, entering), -1)
    own = jnp.concatenate([up_proj[0].T, down_proj[0]], axis=0)
    close = near(own)
    own_other = across(own)
    chip = sender // 2
    held = jnp.stack([chip, chip ^ 1]).astype(jnp.int32)
    router_turned = router[0].T
    router_rows = jnp.concatenate(
        [router_turned, router_turned, jnp.zeros((SLOTS // 2, router_turned.shape[1]), jnp.bfloat16)]
    )
    arriving_there = mirror(after(arriving, own_other, saved_there, held, router_rows))
    entering_there = mirror(jnp.concatenate([entering, listed], axis=0), 0)
    close_other = across(after(close, arriving_there, entering_there))
    pieces = (own, own_other, close, close_other)
    quarter = SLOTS // 4
    kept_bwd, sent_bwd = run_experts(
        backward_kernel,
        held,
        (saved, saved_there, arriving, arriving_there),
        (listed, entering_there),
        norm_gain,
        router_rows,
        pieces,
        3,
        SLOTS,
    )
    came_bwd = mirror(sent_bwd)
    kept_fwd, sent_fwd = run_experts(
        forward_kernel,
        held,
        (entering, after(entering_there, sent_bwd)),
        (listed, entering_there),
        norm_gain,
        router_rows,
        pieces,
        2,
        0,
    )
    came_fwd = mirror(sent_fwd)
    grad_back = run_closing(saved, arriving, norm_gain, kept_bwd, came_bwd)
    terms = sent_bwd[tokens:].astype(jnp.float32) + came_bwd[tokens:].astype(jnp.float32)
    terms = terms[:quarter] + terms[quarter : 2 * quarter]
    devices = lax.axis_size("expert")
    four = devices // 2
    terms = jnp.broadcast_to(terms[None], (four, *terms.shape))
    groups = [[first * four + i for i in range(four)] for first in range(2)]
    terms = lax.all_to_all(
        terms, "expert", split_axis=0, concat_axis=0, tiled=True, axis_index_groups=groups
    )
    summed = jnp.sum(terms, axis=0)
    square = jnp.sum(summed * summed, keepdims=True)
    square = after(jnp.broadcast_to(square, (1, 128)), grad_back)
    total = square
    for by in range(1, lax.axis_size("pipe")):
        total += shift(square, by)
    norm_sq = total[0, 0]
    width = summed.shape[1] // devices
    grad_rows = lax.dynamic_slice_in_dim(summed, sender * width, width, 1).T
    factor = jnp.minimum(1.0, clip_norm / jnp.sqrt(norm_sq))
    clipped = grad_rows * factor
    new_m = beta_first * moment_m[0] + (1.0 - beta_first) * clipped
    new_v = beta_second * moment_v[0] + (1.0 - beta_second) * clipped * clipped
    first_fix = 1.0 - beta_first**STEP
    second_fix = 1.0 - beta_second**STEP
    router_update = new_m / first_fix / (jnp.sqrt(new_v / second_fix) + 1e-08)
    segment_out = (kept_fwd + came_fwd.astype(jnp.float32)).astype(jnp.bfloat16)
    return (
        segment_out[None],
        grad_back[None],
        new_m[None],
        new_v[None],
        router_update[None],
    )


def solution(mesh):
    in_specs = (
        P("pipe", "expert", None),
        P("pipe", "expert", None),
        P("pipe", "expert", None),
        P("pipe", "expert", None),
        P("pipe", "expert", None),
        P("pipe", None),
        P("pipe", None, None),
        P("pipe", None, "expert"),
        P("pipe", "expert", None),
        P("pipe", "expert", None),
        P("pipe", "expert", None),
    )
    out_specs = (
        P("pipe", "expert", None),
        P("pipe", "expert", None),
        P("pipe", "expert", None),
        P("pipe", "expert", None),
        P("pipe", "expert", None),
    )
    experts_held = mesh.shape["expert"] // 2
    return jax.shard_map(
        paired if experts_held == 4 else dispatched, mesh=mesh, in_specs=in_specs, out_specs=out_specs, check_vma=False
    )
```

```python
import math

import jax
import jax.numpy as jnp
from jax import lax
from jax.experimental import pallas as pl
from jax.experimental.pallas import tpu as pltpu
from jax.sharding import PartitionSpec as P

STEP = 10


gelu_scale = math.sqrt(2.0 / math.pi)
beta_first = 0.9
beta_second = 0.95
clip_norm = 1.0


def shifted(x, axis, by):
    length = lax.axis_size(axis)
    return lax.ppermute(x, axis, [(i, (i + by) % length) for i in range(length)])


def from_partner(value, axis, bit):
    mask = 2**bit
    pairs = [(source, source ^ mask) for source in range(lax.axis_size(axis))]
    return lax.ppermute(value, axis, pairs)


def gelu_parts(preact):
    square = preact * preact
    tangent = jnp.tanh(gelu_scale * (preact + 0.044715 * square * preact))
    activated = 0.5 * preact * (1.0 + tangent)
    gelu_slope = 0.5 * (1.0 + tangent) + 0.5 * preact * (1.0 - tangent * tangent) * gelu_scale * (
        1.0 + 0.134145 * square
    )
    return (activated, gelu_slope)


def normalize(inputs, gain_row):
    widened = inputs.astype(jnp.float32)
    inv_rms = lax.rsqrt(jnp.mean(widened * widened, axis=-1, keepdims=True) + 1e-05)
    scaled = widened * inv_rms
    return ((scaled * gain_row).astype(jnp.bfloat16), scaled, inv_rms)


def route_gates(normed, router_table, routes):
    logits = jnp.dot(normed, router_table, preferred_element_type=jnp.float32)
    columns = jnp.arange(router_table.shape[1], dtype=jnp.int32)
    picked = (routes[:, :, None] == columns[None, None, :]).astype(jnp.float32)
    chosen = jnp.sum(logits[:, None, :] * picked, axis=2)
    first_gate = jax.nn.sigmoid(chosen[:, 0] - chosen[:, 1])
    second = jax.nn.sigmoid(chosen[:, 1] - chosen[:, 0])
    return (jnp.stack([first_gate, second], axis=1), picked)


def slot_plan(routes, half_cap, sender):
    flat_routes = routes.reshape(-1)
    rows = jnp.arange(flat_routes.shape[0], dtype=jnp.int32)
    before = (rows[:, None] > rows[None, :]) & (flat_routes[:, None] == flat_routes[None, :])
    position = jnp.sum(before.astype(jnp.int32), axis=1)
    target = 2 * flat_routes + (position + sender) % 2
    return target * half_cap + position // 2


def pack_rows(row_block, slots, slot_total):
    blank_rows = jnp.zeros((slot_total, row_block.shape[1]), row_block.dtype)
    return blank_rows.at[slots].set(row_block)


def transposed(left, right):
    return lax.dot_general(
        left, right, (((1,), (1,)), ((), ())), preferred_element_type=jnp.float32
    )


def expert_forward(pieces, halves):
    own_up, other_up, own_down, other_down = halves
    row_block = pieces.reshape(-1, pieces.shape[-1])
    active_own = gelu_parts(jnp.dot(row_block, own_up, preferred_element_type=jnp.float32))[
        0
    ].astype(jnp.bfloat16)
    active_other = gelu_parts(jnp.dot(row_block, other_up, preferred_element_type=jnp.float32))[
        0
    ].astype(jnp.bfloat16)
    total = jnp.dot(active_own, own_down, preferred_element_type=jnp.float32) + jnp.dot(
        active_other, other_down, preferred_element_type=jnp.float32
    )
    return total.astype(jnp.bfloat16).reshape(pieces.shape)


def expert_backward(pieces, grad_pieces, halves):
    own_up, other_up, own_down, other_down = halves
    row_block = pieces.reshape(-1, pieces.shape[-1])
    grad_rows = grad_pieces.reshape(-1, pieces.shape[-1])
    active_own, slope_own = gelu_parts(
        jnp.dot(row_block, own_up, preferred_element_type=jnp.float32)
    )
    active_other, slope_other = gelu_parts(
        jnp.dot(row_block, other_up, preferred_element_type=jnp.float32)
    )
    total = jnp.dot(
        active_own.astype(jnp.bfloat16), own_down, preferred_element_type=jnp.float32
    ) + jnp.dot(active_other.astype(jnp.bfloat16), other_down, preferred_element_type=jnp.float32)
    back_own = (transposed(grad_rows, own_down) * slope_own).astype(jnp.bfloat16)
    back_other = (transposed(grad_rows, other_down) * slope_other).astype(jnp.bfloat16)
    input_grads = transposed(back_own, own_up) + transposed(back_other, other_up)
    return (
        total.astype(jnp.bfloat16).reshape(pieces.shape),
        input_grads.astype(jnp.bfloat16).reshape(pieces.shape),
    )


def dispatched(
    handoff,
    saved_in,
    grad_handoff,
    route_fwd,
    route_bwd,
    norm_gain,
    router,
    up_proj,
    down_proj,
    moment_m,
    moment_v,
):
    tok_rows = handoff.shape[1]
    feature_dim = handoff.shape[2]
    devices = lax.axis_size("expert")
    experts = devices // 2
    half_cap = max(3, 3 * tok_rows // (2 * experts))
    slot_total = devices * half_cap
    gain_row = norm_gain[0]
    router_table = router[0]
    sender = lax.axis_index("expert")
    entering = shifted(handoff[0], "pipe", 1)
    arriving = shifted(grad_handoff[0], "pipe", -1)
    own_up = up_proj[0]
    own_down = down_proj[0]
    other_up, other_down = from_partner((own_up, own_down), "expert", 0)
    halves = (own_up, other_up, own_down, other_down)
    normed_fwd = normalize(entering, gain_row)[0]
    gates_fwd = route_gates(normed_fwd, router_table, route_fwd[0])[0]
    slots_fwd = slot_plan(route_fwd[0], half_cap, sender)
    send_fwd = pack_rows(jnp.repeat(normed_fwd, 2, axis=0), slots_fwd, slot_total).reshape(
        devices, half_cap, feature_dim
    )
    normed_bwd, scaled_bwd, inv_rms = normalize(saved_in[0], gain_row)
    gates_bwd, picked = route_gates(normed_bwd, router_table, route_bwd[0])
    slots_bwd = slot_plan(route_bwd[0], half_cap, sender)
    send_bwd = pack_rows(jnp.repeat(normed_bwd, 2, axis=0), slots_bwd, slot_total).reshape(
        devices, half_cap, feature_dim
    )
    cotangent = arriving.astype(jnp.float32)
    slot_grads = (
        (gates_bwd[:, :, None] * cotangent[:, None, :])
        .astype(jnp.bfloat16)
        .reshape(-1, feature_dim)
    )
    send_grad = pack_rows(slot_grads, slots_bwd, slot_total).reshape(devices, half_cap, feature_dim)
    back_fwd = lax.all_to_all(
        expert_forward(
            lax.all_to_all(send_fwd, "expert", split_axis=0, concat_axis=0, tiled=True), halves
        ),
        "expert",
        split_axis=0,
        concat_axis=0,
        tiled=True,
    )
    out_second, grad_second = expert_backward(
        lax.all_to_all(send_bwd, "expert", split_axis=0, concat_axis=0, tiled=True),
        lax.all_to_all(send_grad, "expert", split_axis=0, concat_axis=0, tiled=True),
        halves,
    )
    back_bwd = lax.all_to_all(out_second, "expert", split_axis=0, concat_axis=0, tiled=True)
    back_grad = lax.all_to_all(grad_second, "expert", split_axis=0, concat_axis=0, tiled=True)
    out_fwd = (
        back_fwd.reshape(slot_total, feature_dim)[slots_fwd]
        .reshape(tok_rows, 2, feature_dim)
        .astype(jnp.float32)
    )
    segment_sum = (
        entering.astype(jnp.float32)
        + gates_fwd[:, 0:1] * out_fwd[:, 0]
        + gates_fwd[:, 1:2] * out_fwd[:, 1]
    )
    out_bwd = (
        back_bwd.reshape(slot_total, feature_dim)[slots_bwd]
        .reshape(tok_rows, 2, feature_dim)
        .astype(jnp.float32)
    )
    grads_in = (
        back_grad.reshape(slot_total, feature_dim)[slots_bwd]
        .reshape(tok_rows, 2, feature_dim)
        .astype(jnp.float32)
    )
    gate_grads = jnp.sum(cotangent[:, None, :] * out_bwd, axis=2)
    logit_step = gates_bwd[:, 0] * gates_bwd[:, 1] * (gate_grads[:, 0] - gate_grads[:, 1])
    logit_grads = (logit_step[:, None] * (picked[:, 0, :] - picked[:, 1, :])).astype(jnp.bfloat16)
    local_grad = lax.dot_general(
        normed_bwd, logit_grads, (((0,), (0,)), ((), ())), preferred_element_type=jnp.float32
    )
    router_back = transposed(logit_grads, router_table)
    normed_grad = grads_in[:, 0] + grads_in[:, 1] + router_back
    scaled_grad = normed_grad * gain_row
    input_grad = inv_rms * (
        scaled_grad - scaled_bwd * jnp.mean(scaled_grad * scaled_bwd, axis=-1, keepdims=True)
    )
    grad_back = (cotangent + input_grad).astype(jnp.bfloat16)
    row_count = feature_dim // devices
    summed = lax.psum(local_grad, "expert")
    norm_sq = lax.psum(jnp.sum(summed * summed), "pipe")
    grad_rows = lax.dynamic_slice_in_dim(summed, sender * row_count, row_count, 0)
    factor = jnp.minimum(1.0, clip_norm / jnp.sqrt(norm_sq))
    clipped = grad_rows * factor
    new_m = beta_first * moment_m[0] + (1.0 - beta_first) * clipped
    new_v = beta_second * moment_v[0] + (1.0 - beta_second) * clipped * clipped
    first_fix = 1.0 - beta_first**STEP
    second_fix = 1.0 - beta_second**STEP
    router_update = new_m / first_fix / (jnp.sqrt(new_v / second_fix) + 1e-08)
    return (
        segment_sum.astype(jnp.bfloat16)[None],
        grad_back[None],
        new_m[None],
        new_v[None],
        router_update[None],
    )


PIECES = 4
SLOTS = 16
MIB = 2**20


def permuted(value, axes, target):
    sizes = [lax.axis_size(axis) for axis in axes]
    count = math.prod(sizes)
    pairs = []
    for source in range(count):
        place = (source // sizes[-1], source % sizes[-1]) if len(axes) == 2 else (0, source)
        row, column = target(*place)
        pairs.append((source, (row % sizes[0]) * sizes[-1] + column if len(axes) == 2 else column))
    return lax.ppermute(value, axes if len(axes) == 2 else axes[0], pairs)


def normed_rows(block, gain_row):
    widened = block.astype(jnp.float32)
    inv_rms = lax.rsqrt(jnp.mean(widened * widened, axis=-1, keepdims=True) + 1e-05)
    return (widened * inv_rms * gain_row).astype(jnp.bfloat16)


def gates_of(rows, router_rows, routes):
    logits = lax.dot_general(
        rows, router_rows, (((1,), (1,)), ((), ())), preferred_element_type=jnp.float32
    )
    column = lax.broadcasted_iota(jnp.int32, logits.shape, 1)
    first, second = routes[:, 0:1], routes[:, 1:2]
    logit_first = jnp.sum(jnp.where(column == first, logits, 0.0), axis=1, keepdims=True)
    logit_second = jnp.sum(jnp.where(column == second, logits, 0.0), axis=1, keepdims=True)
    gate_first = jax.nn.sigmoid(logit_first - logit_second)
    gate_second = jax.nn.sigmoid(logit_second - logit_first)
    return first, second, gate_first, gate_second


def route_columns(marks, row):
    turned = jnp.concatenate([marks[0], marks[1]], axis=1).astype(jnp.float32).T
    picked = turned[:, row : row + 2].astype(jnp.int32)
    return picked


def weight_loads(pieces, up_all, down_all, arrived):
    width = up_all.shape[0] // PIECES
    ups, downs = [], []
    for i in range(PIECES):
        part = pl.ds(i * width, width)
        ups.append(
            pltpu.make_async_copy(pieces[i].at[pl.ds(0, width)], up_all.at[part], arrived.at[i])
        )
        downs.append(
            pltpu.make_async_copy(
                pieces[i].at[pl.ds(width, width)], down_all.at[part], arrived.at[PIECES + i]
            )
        )
    return width, ups, downs


def pick(first, second, for_first, for_second, expert):
    return jnp.where(first == expert, for_first, 0.0) + jnp.where(
        second == expert, for_second, 0.0
    )


def forward_kernel(held, next_here, next_there, listed, marked, gain, router_rows, *rest):
    pieces = rest[:PIECES]
    kept, sent, up_all, down_all, entered, rows, hidden, marks, arrived, landed = rest[PIECES:]
    tokens = next_here.shape[0]
    lines, lanes = pl.ds(tokens, SLOTS), pl.ds(0, tokens)
    loads = [
        pltpu.make_async_copy(next_here, entered.at[pl.ds(0, tokens)], landed.at[0]),
        pltpu.make_async_copy(next_there.at[pl.ds(0, tokens)], entered.at[pl.ds(tokens, tokens)], landed.at[1]),
        pltpu.make_async_copy(listed.at[:, lanes], marks.at[0], landed.at[2]),
        pltpu.make_async_copy(marked.at[lines, lanes], marks.at[1], landed.at[3]),
    ]
    for load in loads:
        load.start()
    width, ups, downs = weight_loads(pieces, up_all, down_all, arrived)
    ups[0].start()
    for load in loads:
        load.wait()
    ups[1].start()
    ups[2].start()
    routes = route_columns(marks, 0)
    rows[...] = normed_rows(entered[...], gain[...])
    first, second, gate_first, gate_second = gates_of(rows[...], router_rows[...], routes)
    for i in range(PIECES):
        part = slice(i * width, (i + 1) * width)
        ups[i].wait()
        if i == 0:
            ups[PIECES - 1].start()
        downs[i].start()
        preact = transposed(rows[...], up_all[part, :])
        gate = pick(first, second, gate_first, gate_second, held[2 * i // PIECES])
        hidden[:, part] = (gelu_parts(preact)[0] * gate).astype(jnp.bfloat16)
    for down in downs:
        down.wait()
    block = 512
    for start in range(0, kept.shape[1], block):
        part = slice(start, start + block)
        total = jnp.dot(hidden[...], down_all[:, part], preferred_element_type=jnp.float32)
        kept[:, part] = entered[:tokens, part].astype(jnp.float32) + total[:tokens]
        sent[:, part] = total[tokens:].astype(jnp.bfloat16)


def backward_kernel(
    held, saved_here, saved_there, grad_here, grad_there, listed, marked, gain, router_rows, *rest
):
    pieces = rest[:PIECES]
    (
        kept,
        sent,
        up_all,
        down_all,
        saved,
        grads,
        rows,
        backs,
        marks,
        arrived,
        landed,
    ) = rest[PIECES:]
    tokens = saved_here.shape[0]
    lines, lanes = pl.ds(tokens, SLOTS), pl.ds(0, tokens)
    upper, lower = pl.ds(0, tokens), pl.ds(tokens, tokens)
    loads = [
        pltpu.make_async_copy(saved_here, saved.at[upper], landed.at[0]),
        pltpu.make_async_copy(saved_there, saved.at[lower], landed.at[1]),
        pltpu.make_async_copy(grad_here, grads.at[upper], landed.at[2]),
        pltpu.make_async_copy(grad_there, grads.at[lower], landed.at[3]),
        pltpu.make_async_copy(listed.at[:, lanes], marks.at[0], landed.at[4]),
        pltpu.make_async_copy(marked.at[lines, lanes], marks.at[1], landed.at[5]),
    ]
    early, late = loads[:2] + loads[4:], loads[2:4]
    for load in early:
        load.start()
    width, ups, downs = weight_loads(pieces, up_all, down_all, arrived)
    ups[0].start()
    for load in early:
        load.wait()
    for load in late:
        load.start()
    downs[0].start()
    ups[1].start()
    routes = route_columns(marks, 2)
    rows[...] = normed_rows(saved[...], gain[...])
    first, second, gate_first, gate_second = gates_of(rows[...], router_rows[...], routes)
    signed_sum = jnp.zeros_like(gate_first)
    for i in range(PIECES):
        expert = held[2 * i // PIECES]
        part = slice(i * width, (i + 1) * width)
        ups[i].wait()
        preact = transposed(rows[...], up_all[part, :])
        if i == 0:
            for load in late:
                load.wait()
        downs[i].wait()
        if i + 1 < PIECES:
            downs[i + 1].start()
        if i + 2 < PIECES:
            ups[i + 2].start()
        hidden_grad = transposed(grads[...], down_all[part, :])
        active, slope = gelu_parts(preact)
        active = active.astype(jnp.bfloat16).astype(jnp.float32)
        signed_sum += pick(first, second, 1.0, -1.0, expert) * jnp.sum(
            active * hidden_grad, axis=1, keepdims=True
        )
        gate = pick(first, second, gate_first, gate_second, expert)
        backs[:, part] = (hidden_grad * slope * gate).astype(jnp.bfloat16)
    step = gate_first * gate_second * signed_sum
    column = lax.broadcasted_iota(jnp.int32, (2 * tokens, SLOTS), 1)
    expert = jnp.where(column < SLOTS // 4, column, column - SLOTS // 4)
    step = pick(first, second, step, -step, expert)
    coarse = step.astype(jnp.bfloat16).astype(jnp.float32)
    logit_grads = jnp.where(column < SLOTS // 4, coarse, step - coarse)
    logit_grads = jnp.where(column < SLOTS // 2, logit_grads, 0.0).astype(jnp.bfloat16)
    block = 512
    for start in range(0, kept.shape[1], block):
        part = slice(start, start + block)
        parts = lax.dot_general(
            logit_grads,
            rows[:, part],
            (((0,), (0,)), ((), ())),
            preferred_element_type=jnp.float32,
        )
        parts = parts + pltpu.roll(parts, SLOTS - SLOTS // 4, 0)
        high = parts.astype(jnp.bfloat16).astype(jnp.float32)
        low = pltpu.roll(parts - high, SLOTS // 4, 0)
        row = lax.broadcasted_iota(jnp.int32, parts.shape, 0)
        sent[tokens : tokens + SLOTS, part] = jnp.where(
            row < SLOTS // 4, high, low
        ).astype(jnp.bfloat16)
        total = jnp.dot(
            backs[...], up_all[:, part], preferred_element_type=jnp.float32
        ) + jnp.dot(logit_grads, router_rows[:, part], preferred_element_type=jnp.float32)
        kept[:, part] = total[:tokens]
        sent[:tokens, part] = total[tokens:].astype(jnp.bfloat16)


def closing_kernel(saved, arriving, gain, kept, came, out):
    widened = saved[...].astype(jnp.float32)
    inv_rms = lax.rsqrt(jnp.mean(widened * widened, axis=-1, keepdims=True) + 1e-05)
    scaled = widened * inv_rms
    scaled_grad = (kept[...] + came[...].astype(jnp.float32)) * gain[...]
    mean = jnp.mean(scaled_grad * scaled, axis=-1, keepdims=True)
    input_grad = inv_rms * (scaled_grad - scaled * mean)
    out[...] = (arriving[...].astype(jnp.float32) + input_grad).astype(jnp.bfloat16)


def in_hbm(count):
    return [pl.BlockSpec(memory_space=pltpu.HBM)] * count


def in_vmem(count):
    return [pl.BlockSpec(memory_space=pltpu.VMEM)] * count


def run_experts(kernel, held, blocks, lists, gain, router_rows, pieces, matmuls, more_rows):
    tokens, features = blocks[0].shape
    hidden = PIECES * pieces[0].shape[0] // 2
    weights = pltpu.VMEM((hidden, features), jnp.bfloat16)
    rows = pltpu.VMEM((2 * tokens, features), jnp.bfloat16)
    return pl.pallas_call(
        kernel,
        out_shape=(
            jax.ShapeDtypeStruct((tokens, features), jnp.float32),
            jax.ShapeDtypeStruct((tokens + more_rows, features), jnp.bfloat16),
        ),
        in_specs=[pl.BlockSpec(memory_space=pltpu.SMEM)]
        + in_hbm(len(blocks) + 2)
        + in_vmem(2)
        + in_hbm(PIECES),
        out_specs=tuple(in_vmem(2)),
        scratch_shapes=[
            weights,
            weights,
            *[rows] * (len(blocks) // 2 + 1),
            pltpu.VMEM((2 * tokens, hidden), jnp.bfloat16),
            pltpu.VMEM((2, SLOTS, tokens), jnp.bfloat16),
            pltpu.SemaphoreType.DMA((2 * PIECES,)),
            pltpu.SemaphoreType.DMA((len(blocks) + 2,)),
        ],
        compiler_params=pltpu.CompilerParams(vmem_limit_bytes=60 * MIB),
        cost_estimate=pl.CostEstimate(
            flops=4 * matmuls * tokens * features * hidden,
            bytes_accessed=4 * features * hidden + 16 * tokens * features,
            transcendentals=2 * tokens * hidden,
        ),
    )(held, *blocks, *lists, gain, router_rows, *pieces)


def run_closing(saved, arriving, gain, kept, came):
    tokens, features = saved.shape
    block = tokens // 4
    rows = pl.BlockSpec((block, features), lambda i: (i, 0))
    return pl.pallas_call(
        closing_kernel,
        out_shape=jax.ShapeDtypeStruct((tokens, features), jnp.bfloat16),
        grid=(4,),
        in_specs=[
            rows,
            rows,
            pl.BlockSpec((1, features), lambda i: (0, 0)),
            rows,
            rows,
        ],
        out_specs=rows,
        cost_estimate=pl.CostEstimate(
            flops=16 * tokens * features, bytes_accessed=12 * tokens * features, transcendentals=0
        ),
    )(saved, arriving, gain, kept, came)


def after(value, *earlier):
    return lax.optimization_barrier((value, *earlier))[0]


def paired(
    handoff,
    saved_in,
    grad_handoff,
    route_fwd,
    route_bwd,
    norm_gain,
    router,
    up_proj,
    down_proj,
    moment_m,
    moment_v,
):
    def shift(value, by):
        return permuted(value, both, lambda row, place: (row + by, place))

    def mirror(value, by=0):
        if by == 0:
            return permuted(value, line, lambda row, place: (row, place ^ 6))
        return permuted(value, both, lambda row, place: (row + by, place ^ 6))

    def near(value):
        return permuted(value, line, lambda row, place: (row, place ^ 2))

    def across(value):
        return permuted(value, line, lambda row, place: (row, place ^ 1))

    both, line = ("pipe", "expert"), ("expert",)
    sender = lax.axis_index("expert")
    saved, leaving, cotangent = saved_in[0], handoff[0], grad_handoff[0]
    routes = jnp.concatenate([route_fwd[0].T, route_bwd[0].T], axis=0)
    tokens, features = saved.shape
    listed = jnp.pad(
        routes.astype(jnp.bfloat16), ((0, SLOTS - routes.shape[0]), (0, features - tokens))
    )
    saved_there = mirror(saved)
    entering = shift(leaving, 1)
    arriving = shift(after(cotangent, entering), -1)
    own = jnp.concatenate([up_proj[0].T, down_proj[0]], axis=0)
    close = near(own)
    own_other = across(own)
    chip = sender // 2
    held = jnp.stack([chip, chip ^ 1]).astype(jnp.int32)
    router_turned = router[0].T
    router_rows = jnp.concatenate(
        [router_turned, router_turned, jnp.zeros((SLOTS // 2, router_turned.shape[1]), jnp.bfloat16)]
    )
    arriving_there = mirror(after(arriving, saved_there, held, router_rows))
    entering_there = mirror(jnp.concatenate([entering, listed], axis=0), 0)
    close_other = across(after(close, arriving_there, entering_there))
    pieces = (own, own_other, close, close_other)
    quarter = SLOTS // 4
    kept_bwd, sent_bwd = run_experts(
        backward_kernel,
        held,
        (saved, saved_there, arriving, arriving_there),
        (listed, entering_there),
        norm_gain,
        router_rows,
        pieces,
        3,
        SLOTS,
    )
    came_bwd = mirror(sent_bwd)
    kept_fwd, sent_fwd = run_experts(
        forward_kernel,
        held,
        (entering, after(entering_there, sent_bwd)),
        (listed, entering_there),
        norm_gain,
        router_rows,
        pieces,
        2,
        0,
    )
    came_fwd = mirror(sent_fwd)
    grad_back = run_closing(saved, arriving, norm_gain, kept_bwd, came_bwd)
    terms = sent_bwd[tokens:].astype(jnp.float32) + came_bwd[tokens:].astype(jnp.float32)
    terms = terms[:quarter] + terms[quarter : 2 * quarter]
    devices = lax.axis_size("expert")
    four = devices // 2
    terms = jnp.broadcast_to(terms[None], (four, *terms.shape))
    groups = [[first * four + i for i in range(four)] for first in range(2)]
    terms = lax.all_to_all(
        terms, "expert", split_axis=0, concat_axis=0, tiled=True, axis_index_groups=groups
    )
    summed = jnp.sum(terms, axis=0)
    square = jnp.sum(summed * summed, keepdims=True)
    square = after(jnp.broadcast_to(square, (1, 128)), grad_back)
    total = square
    for by in range(1, lax.axis_size("pipe")):
        total += shift(square, by)
    norm_sq = total[0, 0]
    width = summed.shape[1] // devices
    grad_rows = lax.dynamic_slice_in_dim(summed, sender * width, width, 1).T
    factor = jnp.minimum(1.0, clip_norm / jnp.sqrt(norm_sq))
    clipped = grad_rows * factor
    new_m = beta_first * moment_m[0] + (1.0 - beta_first) * clipped
    new_v = beta_second * moment_v[0] + (1.0 - beta_second) * clipped * clipped
    first_fix = 1.0 - beta_first**STEP
    second_fix = 1.0 - beta_second**STEP
    router_update = new_m / first_fix / (jnp.sqrt(new_v / second_fix) + 1e-08)
    segment_out = (kept_fwd + came_fwd.astype(jnp.float32)).astype(jnp.bfloat16)
    return (
        segment_out[None],
        grad_back[None],
        new_m[None],
        new_v[None],
        router_update[None],
    )


def solution(mesh):
    in_specs = (
        P("pipe", "expert", None),
        P("pipe", "expert", None),
        P("pipe", "expert", None),
        P("pipe", "expert", None),
        P("pipe", "expert", None),
        P("pipe", None),
        P("pipe", None, None),
        P("pipe", None, "expert"),
        P("pipe", "expert", None),
        P("pipe", "expert", None),
        P("pipe", "expert", None),
    )
    out_specs = (
        P("pipe", "expert", None),
        P("pipe", "expert", None),
        P("pipe", "expert", None),
        P("pipe", "expert", None),
        P("pipe", "expert", None),
    )
    experts_held = mesh.shape["expert"] // 2
    return jax.shard_map(
        paired if experts_held == 4 else dispatched, mesh=mesh, in_specs=in_specs, out_specs=out_specs, check_vma=False
    )
```
